32 devices in a mesh: frame: 8 (over z, y), coil: 4 (over x, core).
Axes of the slice: x: 2, y: 2, z: 4, core: 2. Of those that a mesh axis runs over, the one named last changes fastest.
Arguments:
- spatial: float32 [8, 2, 320, 320], P(None, None, 'coil', 'frame'), may hold values from -6 to 6
- temporal: float32 [16, 8], P('frame'), may hold values from -2 to 2
- sensitivity: bfloat16 [8, 2, 320, 320], P('coil'), may hold values from -5 to 5
- coil_data: bfloat16 [16, 8, 2, 320, 320], P('frame', 'coil'), may hold values from -6 to 6
- kernel_index: int32 [16, 640, 640], P('frame'), may hold values from 0 to 7
- kernel_level: float32 [16, 8], P('frame'), may hold values from 0.02 to 4
Outputs:
- spatial_next: float32 [8, 2, 320, 320], P(None, None, 'coil', 'frame')
- images: bfloat16 [16, 2, 320, 320], P('frame')
The draws below stay inside these ranges and needn't reach their ends.
All inputs are finite; a program needn't handle non-finite values.
Results may differ from the reference program's by a relative error of at most 0.001.
Values may be sent and summed in bfloat16 or wider, within the bound.
No kernel may reach another device: no remote copies, remote signals or barrier semaphores. Data moves between devices by JAX's collectives and lax.ppermute only.
A program may use at most 128 MiB of HBM per device.

```python
import math
import jax
import jax.numpy as jnp
from jax import lax

NX = 320
NY = 320
COILS = 8
RANK = 8
LEVELS = 8
FRAMES = 16
PX = 640
PY = 640


def plant(entries, stream_key, least, largest):
    extent = entries.shape
    place = [jax.random.randint(jax.random.fold_in(stream_key, axis), (), 0, extent[axis]) for axis in range(len(extent))]
    entries = entries.at[tuple(place)].set(least)
    longest = extent.index(max(extent))
    place[longest] = (place[longest] + 1) % extent[longest]
    return entries.at[tuple(place)].set(largest)


def level_of(key, extent, pieces, low, high):
    factor_of = 1.0
    for position, parts in pieces:
        draws = jax.random.uniform(jax.random.fold_in(jax.random.fold_in(key, 6), position), (parts,), jnp.float32, low / len(pieces), high / len(pieces))
        factor_of = factor_of * jnp.repeat(jnp.exp(draws), extent[position] // parts).reshape((-1,) + (1,) * (len(extent) - 1 - position))
    return factor_of


def normal_values(key, shape, scale, bound, split=(), held_as=jnp.bfloat16):
    factor_of = level_of(key, shape, split, -0.22, 0.18) if split else 1.0
    array = jax.random.normal(key, shape, jnp.float32) * scale * factor_of
    return jnp.minimum(jnp.maximum(array, -bound), bound).astype(held_as)


def setup_inputs(seed: int = 0) -> dict:
    seeds = jax.random.split(jax.random.key(seed), 7)
    spatial = normal_values(seeds[0], (RANK, 2, NX, NY), 1.0, 6.0, ((2, 4), (3, 8)), jnp.float32)
    temporal = normal_values(seeds[1], (FRAMES, RANK), RANK ** -0.5, 2.0, ((0, 8),), jnp.float32)
    sensitivity = normal_values(seeds[2], (COILS, 2, NX, NY), 0.35, 5.0, ((0, 4),))
    coil_data = normal_values(seeds[3], (FRAMES, COILS, 2, NX, NY), 1.0, 6.0, ((0, 8), (1, 4)))
    kernel_index = plant(jax.random.randint(seeds[4], (FRAMES, PX, PY), 0, LEVELS), jax.random.fold_in(seeds[4], 1), 0, LEVELS - 1).astype(jnp.int32)
    kernel_level = jnp.clip(jnp.exp(math.log(4.0) - 5.2983174 * jax.random.uniform(seeds[5], (FRAMES, LEVELS), jnp.float32) ** level_of(seeds[5], (FRAMES, LEVELS), ((0, 8),), -0.2, 0.2)), 0.02, 4.0)
    return dict(spatial=spatial, temporal=temporal, sensitivity=sensitivity, coil_data=coil_data, kernel_index=kernel_index, kernel_level=kernel_level)


STEP_SIZE = 0.15


def rebuild(temporal, factors):
    mixed = jnp.einsum('tr,rcxy->tcxy', temporal, factors, precision=lax.Precision.HIGHEST)
    return mixed.astype(jnp.bfloat16)


def reference(spatial, temporal, sensitivity, coil_data, kernel_index, kernel_level):
    images_old = rebuild(temporal, spatial)
    sens_real = sensitivity[:, 0].astype(jnp.float32)
    sens_imag = sensitivity[:, 1].astype(jnp.float32)

    def residual_frame(items):
        image, data, index, level = items
        img = image.astype(jnp.float32)
        coil_real = sens_real * img[0] - sens_imag * img[1]
        coil_imag = sens_real * img[1] + sens_imag * img[0]
        spectrum = jnp.fft.fft2(coil_real + 1j * coil_imag, s=(PX, PY))
        kernel = level[index]
        back = jnp.fft.ifft2(spectrum * kernel)[:, :NX, :NY]
        diff_real = back.real - data[:, 0].astype(jnp.float32)
        diff_imag = back.imag - data[:, 1].astype(jnp.float32)
        res_real = jnp.sum(sens_real * diff_real + sens_imag * diff_imag, axis=0)
        res_imag = jnp.sum(sens_real * diff_imag - sens_imag * diff_real, axis=0)
        return jnp.stack([res_real, res_imag])

    residual = lax.map(residual_frame, (images_old, coil_data, kernel_index, kernel_level))
    gradient = jnp.einsum('tr,tcxy->rcxy', temporal, residual, precision=lax.Precision.HIGHEST)
    spatial_next = spatial - STEP_SIZE * gradient
    images = rebuild(temporal, spatial_next)
    return spatial_next, images
```

```python
import jax, jax.numpy as jnp, numpy as np
from jax import lax
from jax.sharding import PartitionSpec as P
from jax.experimental import pallas as pl
from jax.experimental.pallas import tpu as pltpu
LANES = 128
F32, BF16 = jnp.float32, jnp.bfloat16


def halves(table):
    high = np.asarray(table, np.float32).astype(BF16)
    low = (table - high.astype(np.float64)).astype(np.float32).astype(BF16)
    return high, low


def wave(count, places, period):
    turns = np.outer(np.arange(count), places) % (2 * period)
    slot = np.outer([period // 2], places) % (2 * period)
    angle = np.pi / period * turns
    cosine, sine = np.cos(angle), np.sin(angle)
    sine[0] = np.sin(np.pi / period * slot[0])
    return cosine, sine


def row_tables(rows, period):
    cosine, sine = wave(rows, 2 * np.arange(rows // 2) + 1, period)
    forward, inverse = [], []
    for table in (cosine, sine):
        high, low = halves(table)
        forward.append(np.concatenate([high, high, low], 1))
        inverse.append(np.concatenate([high.T, high.T, low.T], 1))
    return np.stack(forward), np.stack(inverse)


def col_tables(cols, period):
    main = cols // LANES * LANES
    cosine, sine = wave(cols, 2 * np.arange(cols) - (cols - 1), period)
    mixed = np.concatenate([cosine[:main], sine[:main], cosine[main:], sine[main:]], 0).T
    high, low = halves(mixed)
    blank = np.zeros((cols - main, mixed.shape[1]), BF16)
    forward = np.concatenate([high[:main], high[:main], low[:main], high[main:], high[main:], low[main:], blank], 0)
    high, low = high.T, low.T
    inverse = np.concatenate([high, high, low], 0)
    return forward, inverse


def split(value):
    high = value.astype(BF16)
    return high, (value - high.astype(F32)).astype(BF16)


def dot(left, right):
    return jnp.dot(left, right, preferred_element_type=F32)


def normal_kernel(img_ref, sens_ref, sig_ref, dif_ref, sig0_ref, data_ref, tcol_ref, trow_ref, tback_ref, tlast_ref, rev_ref,
                  out_ref, img_s, xcat, mid, pq, back, last, acc):
    coils, _, rows, wide = sens_ref.shape
    cols = out_ref.shape[2]
    half = rows // 2
    main = cols // LANES * LANES
    spectral = tcol_ref.shape[1]
    steps = spectral // LANES
    for part in range(2):
        for top, value in enumerate((img_ref[part, half:].astype(F32), dot(rev_ref[...], img_ref[part, :half]))):
            here = slice(top * half, top * half + half)
            img_s[part, here, :main] = value[:, :main]
            img_s[part, here, main:] = jnp.concatenate([value[:, main:]] * (LANES // (cols - main)), 1)
    lane = lax.broadcasted_iota(jnp.int32, (half, LANES), 1)
    keep = (lane > 0).astype(F32)
    low_lane = lane < (cols - main)

    def one_coil(coil, carry):
        sums = {}
        for top in range(2):
            here = slice(top * half, top * half + half)
            s_re = sens_ref[coil, 0, here].astype(F32)
            s_im = sens_ref[coil, 1, here].astype(F32)
            i_re, i_im = img_s[0, here], img_s[1, here]
            sums[top, 0] = s_re * i_re - s_im * i_im
            sums[top, 1] = s_re * i_im + s_im * i_re
        for part in range(2):
            for sign in range(2):
                value = sums[0, part] + sums[1, part] if sign == 0 else sums[0, part] - sums[1, part]
                high, low = split(value)
                there = slice((2 * sign + part) * half, (2 * sign + part + 1) * half)
                xcat[there, :main] = high[:, :main]
                xcat[there, main : 2 * main] = low[:, :main]
                xcat[there, 2 * main : 3 * main] = high[:, :main]
                xcat[there, 3 * main : 3 * main + LANES] = jnp.where(low_lane, high[:, main:], low[:, main:])
                xcat[there, 3 * main + LANES :] = high[:, main:]
        for sign in range(2):
            both = dot(xcat[2 * sign * half : (2 * sign + 2) * half], tcol_ref[...])
            re, im = both[:half], both[half:]
            for step in range(steps):
                at = step * LANES
                if at < main:
                    c_re, c_im = re[:, at : at + LANES], im[:, at : at + LANES]
                    s_re, s_im = re[:, main + at : main + at + LANES], im[:, main + at : main + at + LANES]
                    if at == 0:
                        s_re, s_im = s_re * keep, s_im * keep
                    m_re, m_im = c_re + s_im, c_im - s_re
                elif at < 2 * main:
                    c_re, c_im = re[:, at - main : at - main + LANES], im[:, at - main : at - main + LANES]
                    s_re, s_im = re[:, at : at + LANES], im[:, at : at + LANES]
                    if at == main:
                        c_re, c_im = c_re * keep, c_im * keep
                    m_re, m_im = c_re - s_im, c_im + s_re
                else:
                    g_re, g_im = re[:, at : at + LANES], im[:, at : at + LANES]
                    m_re = g_re + pltpu.roll(g_im, LANES // 2, 1)
                    m_im = g_im - pltpu.roll(g_re, LANES // 2, 1)
                for part, value in enumerate((m_re, m_im)):
                    high, low = split(value)
                    there = slice((2 * step + part) * LANES, (2 * step + part + 1) * LANES)
                    mid[sign, :half, there] = high
                    mid[sign, half : 2 * half, there] = low
                    mid[sign, 2 * half :, there] = high

        def one_step(step, carry):
            there = pl.ds(pl.multiple_of(step * 2 * LANES, 2 * LANES), 2 * LANES)
            here = pl.ds(pl.multiple_of(step * LANES, LANES), LANES)
            even = dot(trow_ref[0], mid[0, :, there])
            odd = dot(trow_ref[1], mid[1, :, there])
            sig, dif = sig_ref[:, here], dif_ref[:, here]
            c_re, c_im = even[:, :LANES], even[:, LANES:]
            s_re, s_im = odd[:, :LANES], odd[:, LANES:]
            p_re = sig * c_re + dif * s_im
            p_im = sig * c_im - dif * s_re
            q_re = sig * s_re - dif * c_im
            q_im = sig * s_im + dif * c_re
            first = sig0_ref[:, here]
            q_re = jnp.concatenate([first * s_re[:8] - dif[:8] * c_im[:8], q_re[8:]], 0)
            q_im = jnp.concatenate([first * s_im[:8] + dif[:8] * c_re[:8], q_im[8:]], 0)
            for number, value in enumerate((p_re, p_im, q_re, q_im)):
                high, low = split(value)
                at = slice(number % 2 * LANES, number % 2 * LANES + LANES)
                pq[number // 2, :rows, at] = high
                pq[number // 2, rows : 2 * rows, at] = low
                pq[number // 2, 2 * rows :, at] = high
            back[0, :, there] = dot(tback_ref[0], pq[0])
            back[1, :, there] = dot(tback_ref[1], pq[1])
            return carry

        lax.fori_loop(0, steps, one_step, 0)
        for sign in range(2):
            for step in range(steps):
                at = step * LANES
                def piece(index, part):
                    return back[sign, :, (2 * index + part) * LANES : (2 * index + part + 1) * LANES]
                shift = main // LANES
                if at < main:
                    u_re, u_im = piece(step, 0), piece(step, 1)
                    v_re, v_im = piece(step + shift, 0), piece(step + shift, 1)
                    if at == 0:
                        v_re, v_im = v_re * keep, v_im * keep
                    w_re, w_im = u_re + v_re, u_im + v_im
                elif at < 2 * main:
                    u_re, u_im = piece(step - shift, 0), piece(step - shift, 1)
                    v_re, v_im = piece(step, 0), piece(step, 1)
                    if at == main:
                        u_re, u_im = u_re * keep, u_im * keep
                    w_re, w_im = v_im - u_im, u_re - v_re
                else:
                    g_re, g_im = piece(step, 0), piece(step, 1)
                    w_re = g_re - pltpu.roll(g_im, LANES // 2, 1)
                    w_im = g_im + pltpu.roll(g_re, LANES // 2, 1)
                for part, value in enumerate((w_re, w_im)):
                    high, low = split(value)
                    there = slice((2 * sign + part) * half, (2 * sign + part + 1) * half)
                    last[there, at : at + LANES] = high
                    last[there, spectral + at : spectral + at + LANES] = low
                    last[there, 2 * spectral + at : 2 * spectral + at + LANES] = high
        final = dot(last[...], tlast_ref[...])
        plus_re, plus_im, minus_re, minus_im = [final[n * half : (n + 1) * half] for n in range(4)]
        for top in range(2):
            here = slice(top * half, top * half + half)
            n_re = plus_re + minus_re if top == 0 else plus_re - minus_re
            n_im = plus_im + minus_im if top == 0 else plus_im - minus_im
            s_re = sens_ref[coil, 0, here, :cols].astype(F32)
            s_im = sens_ref[coil, 1, here, :cols].astype(F32)
            acc[0, here] += s_re * n_re + s_im * n_im
            acc[1, here] += s_re * n_im - s_im * n_re
        return carry

    acc[...] = jnp.zeros_like(acc)
    lax.fori_loop(0, coils, one_coil, 0)
    for part in range(2):
        out_ref[part, half:] = acc[part, :half] - data_ref[part, half:]
        below = acc[part, half:]
        high, low = split(below)
        rest = (below - high.astype(F32) - low.astype(F32)).astype(BF16)
        turned = dot(rev_ref[...], high) + dot(rev_ref[...], low) + dot(rev_ref[...], rest)
        out_ref[part, :half] = turned - data_ref[part, :half]


def normal_call(img, sens, sig, dif, sig0, data, tables):
    rows, cols = img.shape[1], data.shape[2]
    half = rows // 2
    tcol, tlast, trow, tback, rev = tables
    spectral = tcol.shape[1]
    return pl.pallas_call(
        normal_kernel,
        out_shape=jax.ShapeDtypeStruct((2, rows, cols), F32),
        in_specs=[pl.BlockSpec(memory_space=pltpu.VMEM)] * 11,
        out_specs=pl.BlockSpec(memory_space=pltpu.VMEM),
        scratch_shapes=[
            pltpu.VMEM((2, rows, sens.shape[3]), F32),
            pltpu.VMEM((4 * half, tcol.shape[0]), BF16),
            pltpu.VMEM((2, 3 * half, 2 * spectral), BF16),
            pltpu.VMEM((2, 3 * rows, 2 * LANES), BF16),
            pltpu.VMEM((2, half, 2 * spectral), F32),
            pltpu.VMEM((4 * half, tlast.shape[0]), BF16),
            pltpu.VMEM((2, rows, cols), F32),
        ],
        compiler_params=pltpu.CompilerParams(vmem_limit_bytes=48 * 1024 * 1024),
    )(img, sens, sig, dif, sig0, data, tcol, trow, tback, tlast, rev)


def freq_order_rows(rows, period):
    k = np.arange(rows)
    return np.concatenate([k, np.where(k == 0, period // 2, period - k)])


def freq_order_cols(cols, period):
    main = cols // LANES * LANES
    l = np.arange(cols)
    u, v = l, np.where(l == 0, period // 2, period - l)
    return np.concatenate([u[:main], v[:main], u[main:], v[main:]])


def prepare_kernel(index_ref, level_ref, sens_ref, row_ref, col_ref, rev_ref, dup_ref, sig_ref, dif_ref, sig0_ref, out_ref):
    frame = pl.program_id(0)
    rows = sig_ref.shape[1]
    half = rows // 2
    levels = level_ref.shape[1]
    scale = 1.0 / (index_ref.shape[1] * index_ref.shape[2])

    def values(index):
        place = dot(index, col_ref[...])
        kernel = jnp.full(place.shape, level_ref[frame, 0] * scale, F32)
        for number in range(1, levels):
            kernel = jnp.where(place > number - 0.5, level_ref[frame, number] * scale, kernel)
        return kernel

    upper = values(index_ref[0, :rows].astype(F32).astype(BF16))
    turned = dot(row_ref[...], index_ref[0, rows:].astype(F32).astype(BF16))
    lower = values(turned.astype(BF16))
    first = lax.broadcasted_iota(jnp.int32, upper[:8].shape, 0) == 0
    sig_ref[0] = upper + lower
    dif_ref[0] = upper - lower
    sig_ref[0, :8] = jnp.where(first, upper[:8], upper[:8] + lower[:8])
    sig0_ref[0] = jnp.where(first, lower[:8], upper[:8] + lower[:8])
    dif_ref[0, :8] = jnp.where(first, 0.0, upper[:8] - lower[:8])

    for part in range(2):
        wide = dot(sens_ref[0, part], dup_ref[...]).astype(BF16)
        out_ref[0, part, :half] = wide[half:]
        out_ref[0, part, half:] = dot(rev_ref[...], wide[:half]).astype(BF16)


def prepare_call(index, level, sens, perms):
    frames, rows_pad, cols_pad = index.shape
    coils, _, rows, cols = sens.shape
    row, col, rev, dup = perms
    whole = lambda n: (lambda f: (0,) * n)
    block = lambda *shape: pl.BlockSpec((1,) + shape, lambda f: (f,) + (0,) * len(shape))
    return pl.pallas_call(
        prepare_kernel,
        grid=(frames,),
        out_shape=(
            jax.ShapeDtypeStruct((frames, rows, cols_pad), F32),
            jax.ShapeDtypeStruct((frames, rows, cols_pad), F32),
            jax.ShapeDtypeStruct((frames, 8, cols_pad), F32),
            jax.ShapeDtypeStruct((coils, 2, rows, dup.shape[1]), BF16),
        ),
        in_specs=[
            block(rows_pad, cols_pad),
            pl.BlockSpec(memory_space=pltpu.SMEM),
            block(2, rows, cols),
            pl.BlockSpec(row.shape, whole(2)),
            pl.BlockSpec(col.shape, whole(2)),
            pl.BlockSpec(rev.shape, whole(2)),
            pl.BlockSpec(dup.shape, whole(2)),
        ],
        out_specs=(block(rows, cols_pad), block(rows, cols_pad), block(8, cols_pad), block(2, rows, dup.shape[1])),
        compiler_params=pltpu.CompilerParams(vmem_limit_bytes=40 * 1024 * 1024),
    )(index, level, sens, row, col, rev, dup)


STEP_SIZE = 0.15


def one_hot(order):
    return (order[:, None] == np.arange(len(order))[None, :]).astype(BF16)


def constants(rows, cols, rows_pad, cols_pad):
    assert rows_pad == 2 * rows and cols_pad == 2 * cols
    main = cols // LANES * LANES
    assert 2 * (cols - main) == LANES and rows % 32 == 0
    forward, inverse = row_tables(rows, rows_pad)
    first, last = col_tables(cols, cols_pad)
    turn = np.arange(rows // 2)[::-1]
    flip = freq_order_rows(rows, rows_pad)[rows:] - rows
    spread = np.concatenate([np.arange(cols), np.arange(main, cols)])
    rev, row = one_hot(turn), one_hot(flip)
    col = one_hot(freq_order_cols(cols, cols_pad)).T
    dup = (np.arange(cols)[:, None] == spread[None, :]).astype(BF16)
    tables = [jnp.asarray(t) for t in (first, last, forward, inverse, rev)]
    return tables, [jnp.asarray(t) for t in (row, col, rev, dup)]


def exchange(value, axis, distance):
    size = lax.axis_size(axis)
    return lax.ppermute(value, axis, [(i, i ^ distance) for i in range(size)])


def gather_rows(block, axis):
    size = lax.axis_size(axis)
    me = lax.axis_index(axis)
    held = block[:, :, None]
    distance = size // 2
    while distance:
        other = exchange(held, axis, distance)
        upper = (me // distance) % 2 == 1
        low = jnp.where(upper, other, held)
        high = jnp.where(upper, held, other)
        held = jnp.stack([low, high], 2).reshape(held.shape[:2] + (2 * held.shape[2],) + held.shape[3:])
        distance //= 2
    bits = size.bit_length() - 1
    lead, shape = held.shape[:2], held.shape[3:]
    held = held.reshape(lead + (2,) * bits + shape)
    order = (0, 1) + tuple(1 + bits - n for n in range(bits)) + (2 + bits, 3 + bits)
    return held.transpose(order).reshape(lead + (size * shape[0], shape[1]))


def scatter_rows(partial, axis):
    size = lax.axis_size(axis)
    me = lax.axis_index(axis)
    count = partial.shape[1] // size
    held = partial.reshape((partial.shape[0], size, count, partial.shape[2]))
    distance = 1
    while distance < size:
        bit = (me // distance) % 2
        paired = held.reshape((held.shape[0], held.shape[1] // 2, 2) + held.shape[2:])
        mine = lax.dynamic_index_in_dim(paired, bit, 2, keepdims=False)
        theirs = lax.dynamic_index_in_dim(paired, 1 - bit, 2, keepdims=False)
        held = mine + exchange(theirs, axis, distance)
        distance *= 2
    return held[:, 0]


def send_images(factors, temporal_all):
    images = jnp.einsum("tr,rcxy->tcxy", temporal_all, factors, precision=lax.Precision.HIGHEST).astype(BF16)
    rows = lax.all_to_all(images, "frame", split_axis=0, concat_axis=3, tiled=True)
    return gather_rows(rows, "coil")


def body(spatial, temporal, sensitivity, coil_data, kernel_index, kernel_level):
    frames = lax.axis_size("frame")
    rows, cols = sensitivity.shape[2:]
    tables, perms = constants(rows, cols, kernel_index.shape[1], kernel_index.shape[2])
    spread = jnp.broadcast_to(temporal[None], (frames,) + temporal.shape)
    temporal_all = lax.all_to_all(spread, "frame", split_axis=0, concat_axis=0, tiled=True)
    temporal_all = temporal_all.reshape((-1, temporal.shape[1]))
    images = send_images(spatial, temporal_all)

    sig, dif, sig0, wide = prepare_call(kernel_index, kernel_level, sensitivity, perms)
    sens_real, sens_imag = sensitivity[:, 0].astype(F32), sensitivity[:, 1].astype(F32)
    data_real, data_imag = coil_data[:, :, 0].astype(F32), coil_data[:, :, 1].astype(F32)
    data = jnp.stack([
        jnp.sum(sens_real * data_real + sens_imag * data_imag, axis=1),
        jnp.sum(sens_real * data_imag - sens_imag * data_real, axis=1),
    ], 1)

    residual = []
    for frame in range(images.shape[0]):
        partial = normal_call(images[frame], wide, sig[frame], dif[frame], sig0[frame], data[frame], tables)
        residual.append(scatter_rows(partial, "coil"))
    residual = lax.all_to_all(jnp.stack(residual), "frame", split_axis=3, concat_axis=0, tiled=True)
    gradient = jnp.einsum("tr,tcxy->rcxy", temporal_all, residual, precision=lax.Precision.HIGHEST)
    spatial_next = spatial - STEP_SIZE * gradient
    return spatial_next, send_images(spatial_next, temporal_all)


def solution(mesh):
    placed = (
        P(None, None, "coil", "frame"),
        P("frame", None),
        P("coil", None, None, None),
        P("frame", "coil", None, None, None),
        P("frame", None, None),
        P("frame", None),
    )
    return jax.shard_map(
        body,
        mesh=mesh,
        in_specs=placed,
        out_specs=(P(None, None, "coil", "frame"), P("frame", None, None, None)),
        check_vma=False,
    )
```

```python
import functools
import jax, jax.numpy as jnp, numpy as np
from jax import lax
from jax.sharding import PartitionSpec as P
from jax.experimental import pallas as pl
from jax.experimental.pallas import tpu as pltpu

LANES = 128
VMEM_BYTES = 67043328
F32, BF16 = jnp.float32, jnp.bfloat16


def halves(table):
    high = np.asarray(table, np.float32).astype(BF16)
    low = (table - high.astype(np.float64)).astype(np.float32).astype(BF16)
    return high, low


def wave(count, places, period):
    turns = np.outer(np.arange(count), places) % (2 * period)
    slot = np.outer([period // 2], places) % (2 * period)
    angle = np.pi / period * turns
    cosine, sine = np.cos(angle), np.sin(angle)
    sine[0] = np.sin(np.pi / period * slot[0])
    return cosine, sine


def row_tables(rows, period):
    cosine, sine = wave(rows, 2 * np.arange(rows // 2) + 1, period)
    forward, inverse = [], []
    for table in (cosine, sine):
        high, low = halves(table)
        forward.append(np.concatenate([high, high, low], 1))
        inverse.append(np.concatenate([high.T, high.T, low.T], 1))
    return np.stack(forward), np.stack(inverse)


def col_tables(cols, period):
    main = cols // LANES * LANES
    cosine, sine = wave(cols, 2 * np.arange(cols) - (cols - 1), period)
    mixed = np.concatenate([cosine[:main], sine[:main], cosine[main:], sine[main:]], 0).T
    high, low = halves(mixed)
    blank = np.zeros((cols - main, mixed.shape[1]), BF16)
    forward = np.concatenate([high[:main], high[:main], low[:main], high[main:], high[main:], low[main:], blank], 0)
    high, low = high.T, low.T
    inverse = np.concatenate([high, high, low], 0)
    return forward, inverse


def split(value):
    high = value.astype(BF16)
    return high, (value - high.astype(F32)).astype(BF16)


def dot(left, right):
    return jnp.dot(left, right, preferred_element_type=F32)


def normal_kernel(size, extra, frame, first_coil, me_ref, *refs):
    parts, refs = refs[:size], refs[size:]
    sens_hbm, sig_hbm, dif_hbm, data_hbm, tcol_hbm, trow_hbm, tback_hbm, tlast_hbm, sig0_ref, rev_ref = refs[:10]
    before, refs = refs[10 : 10 + extra], refs[10 + extra :]
    blocks, refs = refs[:size], refs[size:]
    sens_ref, tcol_ref, trow_ref, sig_ref, dif_ref, tback_ref, tlast_ref, data_ref, sems = refs[:9]
    img_n, img_s, xcat, mid, back, last, acc = refs[9:]
    chosen = pl.ds(first_coil, sens_ref.shape[0])
    moved = [
        pltpu.make_async_copy(source, target, sems.at[n])
        for n, (source, target) in enumerate((
            (sens_hbm.at[chosen], sens_ref), (tcol_hbm, tcol_ref), (trow_hbm, trow_ref), (sig_hbm.at[frame], sig_ref), (dif_hbm.at[frame], dif_ref),
            (tback_hbm, tback_ref), (tlast_hbm, tlast_ref), (data_hbm.at[frame, chosen], data_ref),
        ))
    ]
    for copy in moved:
        copy.start()
    coils, _, rows, _ = sens_ref.shape
    cols = acc.shape[2]
    half = rows // 2
    main = cols // LANES * LANES
    spectral = tcol_ref.shape[1]
    steps = spectral // LANES
    count = rows // size

    def place(number):
        return pl.ds(pl.multiple_of((me_ref[0] ^ number) * count, count), count)

    for number in range(size):
        for part in range(2):
            img_n[part, place(number)] = parts[number][part]
    for part in range(2):
        for top, value in enumerate((img_n[part, half:].astype(F32), dot(rev_ref[...], img_n[part, :half]))):
            here = slice(top * half, top * half + half)
            img_s[part, here, :main] = value[:, :main]
            img_s[part, here, main:] = jnp.concatenate([value[:, main:]] * (LANES // (cols - main)), 1)
    moved[0].wait()
    lane = lax.broadcasted_iota(jnp.int32, (half, LANES), 1)
    keep = (lane > 0).astype(F32)
    low_lane = lane < (cols - main)

    def one_coil(coil, carry):
        sums = {}
        for top in range(2):
            here = slice(top * half, top * half + half)
            s_re = sens_ref[coil, 0, here].astype(F32)
            s_im = sens_ref[coil, 1, here].astype(F32)
            i_re, i_im = img_s[0, here], img_s[1, here]
            sums[top, 0] = s_re * i_re - s_im * i_im
            sums[top, 1] = s_re * i_im + s_im * i_re
        for part in range(2):
            for sign in range(2):
                value = sums[0, part] + sums[1, part] if sign == 0 else sums[0, part] - sums[1, part]
                high, low = split(value)
                there = slice((2 * sign + part) * half, (2 * sign + part + 1) * half)
                xcat[there, :main] = high[:, :main]
                xcat[there, main : 2 * main] = low[:, :main]
                xcat[there, 2 * main : 2 * main + LANES] = jnp.where(low_lane, high[:, main:], low[:, main:])
                xcat[there, 2 * main + LANES :] = high[:, main:]

        @pl.when(coil == 0)
        def _():
            moved[1].wait()

        for sign in range(2):
            lines = slice(2 * sign * half, (2 * sign + 2) * half)
            spread = [xcat[lines, : 2 * main], xcat[lines, :main], xcat[lines, 2 * main :]]
            both = dot(jnp.concatenate(spread, 1), tcol_ref[...])
            re, im = both[:half], both[half:]
            for step in range(steps):
                at = step * LANES
                if at < main:
                    c_re, c_im = re[:, at : at + LANES], im[:, at : at + LANES]
                    s_re, s_im = re[:, main + at : main + at + LANES], im[:, main + at : main + at + LANES]
                    if at == 0:
                        s_re, s_im = s_re * keep, s_im * keep
                    m_re, m_im = c_re + s_im, c_im - s_re
                elif at < 2 * main:
                    c_re, c_im = re[:, at - main : at - main + LANES], im[:, at - main : at - main + LANES]
                    s_re, s_im = re[:, at : at + LANES], im[:, at : at + LANES]
                    if at == main:
                        c_re, c_im = c_re * keep, c_im * keep
                    m_re, m_im = c_re - s_im, c_im + s_re
                else:
                    g_re, g_im = re[:, at : at + LANES], im[:, at : at + LANES]
                    m_re = g_re + pltpu.roll(g_im, LANES // 2, 1)
                    m_im = g_im - pltpu.roll(g_re, LANES // 2, 1)
                for part, value in enumerate((m_re, m_im)):
                    high, low = split(value)
                    there = slice((2 * step + part) * LANES, (2 * step + part + 1) * LANES)
                    mid[sign, :half, there] = high
                    mid[sign, half:, there] = low

        @pl.when(coil == 0)
        def _():
            for copy in moved[2:6]:
                copy.wait()

        def one_step(step, carry):
            there = pl.ds(pl.multiple_of(step * 2 * LANES, 2 * LANES), 2 * LANES)
            here = pl.ds(pl.multiple_of(step * LANES, LANES), LANES)
            even, odd = [
                dot(trow_ref[sign], jnp.concatenate([mid[sign, :, there], mid[sign, :half, there]], 0)) for sign in range(2)
            ]
            sig, dif = sig_ref[:, here], dif_ref[:, here]
            c_re, c_im = even[:, :LANES], even[:, LANES:]
            s_re, s_im = odd[:, :LANES], odd[:, LANES:]
            p_re = sig * c_re + dif * s_im
            p_im = sig * c_im - dif * s_re
            q_re = sig * s_re - dif * c_im
            q_im = sig * s_im + dif * c_re
            first = sig0_ref[frame, :, here]
            q_re = jnp.concatenate([first * s_re[:8] - dif[:8] * c_im[:8], q_re[8:]], 0)
            q_im = jnp.concatenate([first * s_im[:8] + dif[:8] * c_re[:8], q_im[8:]], 0)
            for number, pair in enumerate(((p_re, p_im), (q_re, q_im))):
                both = [split(value) for value in pair]
                high, low = [jnp.concatenate([both[0][n], both[1][n]], 1) for n in range(2)]
                back[number, :, there] = dot(tback_ref[number], jnp.concatenate([high, low, high], 0))
            return carry

        lax.fori_loop(0, steps, one_step, 0, unroll=True)
        for sign in range(2):
            for step in range(steps):
                at = step * LANES

                def piece(index, part):
                    return back[sign, :, (2 * index + part) * LANES : (2 * index + part + 1) * LANES]

                shift = main // LANES
                if at < main:
                    u_re, u_im = piece(step, 0), piece(step, 1)
                    v_re, v_im = piece(step + shift, 0), piece(step + shift, 1)
                    if at == 0:
                        v_re, v_im = v_re * keep, v_im * keep
                    w_re, w_im = u_re + v_re, u_im + v_im
                elif at < 2 * main:
                    u_re, u_im = piece(step - shift, 0), piece(step - shift, 1)
                    v_re, v_im = piece(step, 0), piece(step, 1)
                    if at == main:
                        u_re, u_im = u_re * keep, u_im * keep
                    w_re, w_im = v_im - u_im, u_re - v_re
                else:
                    g_re, g_im = piece(step, 0), piece(step, 1)
                    w_re = g_re - pltpu.roll(g_im, LANES // 2, 1)
                    w_im = g_im + pltpu.roll(g_re, LANES // 2, 1)
                for part, value in enumerate((w_re, w_im)):
                    high, low = split(value)
                    there = slice((2 * sign + part) * half, (2 * sign + part + 1) * half)
                    last[there, at : at + LANES] = high
                    last[there, spectral + at : spectral + at + LANES] = low

        @pl.when(coil == 0)
        def _():
            moved[6].wait()
            moved[7].wait()

        final = dot(jnp.concatenate([last[...], last[:, :spectral]], 1), tlast_ref[...])
        plus_re, plus_im, minus_re, minus_im = [final[n * half : (n + 1) * half] for n in range(4)]
        for top in range(2):
            here = slice(top * half, top * half + half)
            n_re = plus_re + minus_re if top == 0 else plus_re - minus_re
            n_im = plus_im + minus_im if top == 0 else plus_im - minus_im
            if top == 0:
                d_re, d_im = data_ref[coil, 0, half:].astype(F32), data_ref[coil, 1, half:].astype(F32)
            else:
                d_re, d_im = dot(rev_ref[...], data_ref[coil, 0, :half]), dot(rev_ref[...], data_ref[coil, 1, :half])
            n_re, n_im = n_re - d_re, n_im - d_im
            s_re = sens_ref[coil, 0, here, :cols].astype(F32)
            s_im = sens_ref[coil, 1, here, :cols].astype(F32)
            acc[0, here] += s_re * n_re + s_im * n_im
            acc[1, here] += s_re * n_im - s_im * n_re
        return carry

    acc[...] = jnp.zeros_like(acc)
    lax.fori_loop(0, coils, one_coil, 0)
    for part in range(2):
        above, below = acc[part, :half], acc[part, half:]
        high, low = split(below)
        rest = (below - high.astype(F32) - low.astype(F32)).astype(BF16)
        turned = dot(rev_ref[...], high) + dot(rev_ref[...], low) + dot(rev_ref[...], rest)
        acc[part, half:] = above
        acc[part, :half] = turned
    for number in range(size):
        for part in range(2):
            value = acc[part, place(number)]
            blocks[number][part] = value + before[number][part] if extra == size else value


def normal_call(frame, chosen, me, parts, sens, sig, dif, sig0, data, tables, before):
    size = len(parts)
    rows, wide = sens.shape[2:]
    coils = len(chosen)
    cols = data.shape[4]
    half = rows // 2
    tcol, tlast, trow, tback, rev = tables
    spectral = tcol.shape[1]
    held = pl.BlockSpec(memory_space=pltpu.VMEM)
    away = pl.BlockSpec(memory_space=pl.ANY)
    like = lambda value: pltpu.VMEM(value.shape, value.dtype)
    one = lambda value: pltpu.VMEM(value.shape[1:], value.dtype)
    some = lambda value: pltpu.VMEM((coils,) + value.shape[1:], value.dtype)
    flops = 2 * coils * 2 * 12 * rows * cols * spectral

    return pl.pallas_call(
        functools.partial(normal_kernel, size, len(before), frame, chosen[0]),
        out_shape=[jax.ShapeDtypeStruct((2, rows // size, cols), F32)] * size,
        in_specs=[pl.BlockSpec(memory_space=pltpu.SMEM)] + [held] * size + [away] * 8 + [held] * 2 + [held if len(before) == size else away] * len(before),
        out_specs=[held] * size,
        scratch_shapes=[
            some(sens), like(tcol), like(trow), one(sig), one(dif), like(tback), like(tlast), some(one(data)),
            pltpu.SemaphoreType.DMA((8,)),
            pltpu.VMEM((2, rows, cols), BF16),
            pltpu.VMEM((2, rows, wide), F32),
            pltpu.VMEM((4 * half, tcol.shape[0] * 3 // 4), BF16),
            pltpu.VMEM((2, 2 * half, 2 * spectral), BF16),
            pltpu.VMEM((2, half, 2 * spectral), F32),
            pltpu.VMEM((4 * half, 2 * spectral), BF16),
            pltpu.VMEM((2, rows, cols), F32),
        ],
        compiler_params=pltpu.CompilerParams(vmem_limit_bytes=VMEM_BYTES),
        cost_estimate=pl.CostEstimate(flops=flops, bytes_accessed=8 * 1024 * 1024, transcendentals=0),
    )(me, *parts, sens, sig, dif, data, tcol, trow, tback, tlast, sig0, rev, *before)


def place_kernel(me_ref, *refs):
    size = len(refs) - 1
    parts, out_ref = refs[:size], refs[size]
    count = parts[0].shape[2]
    for number in range(size):
        for frame in range(out_ref.shape[0]):
            for part in range(2):
                there = pl.ds(pl.multiple_of((me_ref[0] ^ number) * count, count), count)
                out_ref[frame, part, there] = parts[number][frame, part]


def place_call(me, parts):
    frames, _, count, cols = parts[0].shape
    held = pl.BlockSpec(memory_space=pltpu.VMEM)
    return pl.pallas_call(
        place_kernel,
        out_shape=jax.ShapeDtypeStruct((frames, 2, count * len(parts), cols), parts[0].dtype),
        in_specs=[pl.BlockSpec(memory_space=pltpu.SMEM)] + [held] * len(parts),
        out_specs=held,
    )(me, *parts)


def freq_order_rows(rows, period):
    k = np.arange(rows)
    return np.concatenate([k, np.where(k == 0, period // 2, period - k)])


def freq_order_cols(cols, period):
    main = cols // LANES * LANES
    l = np.arange(cols)
    u, v = l, np.where(l == 0, period // 2, period - l)
    return np.concatenate([u[:main], v[:main], u[main:], v[main:]])


def prepare_kernel(index_ref, level_ref, sens_ref, row_ref, col_ref, rev_ref, dup_ref, after_ref, sig_ref, dif_ref, sig0_ref, out_ref):
    frame = pl.program_id(0)
    rows = sig_ref.shape[1]
    half = rows // 2
    levels = level_ref.shape[1]
    scale = 1.0 / (index_ref.shape[1] * index_ref.shape[2])

    def values(index):
        place = dot(index, col_ref[...])
        kernel = jnp.full(place.shape, level_ref[frame, 0] * scale, F32)
        for number in range(1, levels):
            kernel = jnp.where(place > number - 0.5, level_ref[frame, number] * scale, kernel)
        return kernel

    upper = values(index_ref[0, :rows].astype(F32).astype(BF16))
    turned = dot(row_ref[...], index_ref[0, rows:].astype(F32).astype(BF16))
    lower = values(turned.astype(BF16))
    first = lax.broadcasted_iota(jnp.int32, upper[:8].shape, 0) == 0
    sig_ref[0] = upper + lower
    dif_ref[0] = upper - lower
    sig_ref[0, :8] = jnp.where(first, upper[:8], upper[:8] + lower[:8])
    sig0_ref[0] = jnp.where(first, lower[:8], upper[:8] + lower[:8])
    dif_ref[0, :8] = jnp.where(first, 0.0, upper[:8] - lower[:8])

    for part in range(2):
        wide = dot(sens_ref[0, part], dup_ref[...]).astype(BF16)
        out_ref[0, part, :half] = wide[half:]
        out_ref[0, part, half:] = dot(rev_ref[...], wide[:half]).astype(BF16)


def prepare_call(index, level, sens, perms, after):
    frames, rows_pad, cols_pad = index.shape
    coils, _, rows, cols = sens.shape
    row, col, rev, dup = perms
    whole = lambda n: (lambda f: (0,) * n)
    block = lambda *shape: pl.BlockSpec((1,) + shape, lambda f: (f,) + (0,) * len(shape))
    return pl.pallas_call(
        prepare_kernel,
        grid=(frames,),
        out_shape=(
            jax.ShapeDtypeStruct((frames, rows, cols_pad), F32),
            jax.ShapeDtypeStruct((frames, rows, cols_pad), F32),
            jax.ShapeDtypeStruct((frames, 8, cols_pad), F32),
            jax.ShapeDtypeStruct((coils, 2, rows, dup.shape[1]), BF16),
        ),
        in_specs=[
            block(rows_pad, cols_pad),
            pl.BlockSpec(memory_space=pltpu.SMEM),
            block(2, rows, cols),
            pl.BlockSpec(row.shape, whole(2)),
            pl.BlockSpec(col.shape, whole(2)),
            pl.BlockSpec(rev.shape, whole(2)),
            pl.BlockSpec(dup.shape, whole(2)),
            pl.BlockSpec(memory_space=pl.ANY),
        ],
        out_specs=(block(rows, cols_pad), block(rows, cols_pad), block(8, cols_pad), block(2, rows, dup.shape[1])),
        compiler_params=pltpu.CompilerParams(vmem_limit_bytes=VMEM_BYTES),
        cost_estimate=pl.CostEstimate(flops=6 * frames * rows * cols_pad * cols_pad, bytes_accessed=16 * 1024 * 1024, transcendentals=0),
    )(index, level, sens, row, col, rev, dup, after)


STEP_SIZE = 0.15


def one_hot(order):
    return (order[:, None] == np.arange(len(order))[None, :]).astype(BF16)


def constants(rows, cols, rows_pad, cols_pad):
    assert rows_pad == 2 * rows and cols_pad == 2 * cols
    main = cols // LANES * LANES
    assert 2 * (cols - main) == LANES and rows % 32 == 0
    forward, inverse = row_tables(rows, rows_pad)
    first, last = col_tables(cols, cols_pad)
    turn = np.arange(rows // 2)[::-1]
    flip = freq_order_rows(rows, rows_pad)[rows:] - rows
    spread = np.concatenate([np.arange(cols), np.arange(main, cols)])
    rev, row = one_hot(turn), one_hot(flip)
    col = one_hot(freq_order_cols(cols, cols_pad)).T
    dup = (np.arange(cols)[:, None] == spread[None, :]).astype(BF16)
    tables = [jnp.asarray(t) for t in (first, last, forward, inverse, rev)]
    return tables, [jnp.asarray(t) for t in (row, col, rev, dup)]


def exchange(value, axis, distance):
    size = lax.axis_size(axis)
    return lax.ppermute(value, axis, [(i, i ^ distance) for i in range(size)])


def gather_blocks(own, axis):
    held = {0: own}
    distance = lax.axis_size(axis) // 2
    while distance:
        for key in list(held):
            held[key ^ distance] = exchange(held[key], axis, distance)
        distance //= 2
    return [held[key] for key in sorted(held)]


def gather_direct(own, axis):
    return [own] + [exchange(own, axis, distance) for distance in range(1, lax.axis_size(axis))]


def scatter_blocks(blocks, axis):
    held = dict(enumerate(blocks))
    distance = 1
    while distance < lax.axis_size(axis):
        held = {
            key: value + exchange(held[key ^ distance], axis, distance)
            for key, value in held.items()
            if not key & distance
        }
        distance *= 2
    return held[0]


def scatter_direct(blocks, axis):
    total = blocks[0]
    for distance in range(1, lax.axis_size(axis)):
        total = total + exchange(blocks[distance], axis, distance)
    return total


def gather_small(value, axis):
    size = lax.axis_size(axis)
    me = lax.axis_index(axis)
    held = value[None]
    distance = 1
    while distance < size:
        other = exchange(held, axis, distance)
        upper = (me // distance) % 2 == 1
        held = jnp.where(upper, jnp.concatenate([other, held]), jnp.concatenate([held, other]))
        distance *= 2
    return held


def make_images(factors, temporal_all):
    mixed = jnp.einsum("ftr,rcxy->ftcxy", temporal_all, factors, precision=lax.Precision.HIGHEST)
    return mixed.astype(BF16)


def send_images(images):
    images = images.reshape((-1,) + images.shape[2:])
    return lax.all_to_all(images, "frame", split_axis=0, concat_axis=3, tiled=True)


def send_residual(value):
    return lax.all_to_all(value[None], "frame", split_axis=3, concat_axis=0, tiled=True)


def body(spatial, temporal, sensitivity, coil_data, kernel_index, kernel_level):
    rows, cols = sensitivity.shape[2:]
    tables, perms = constants(rows, cols, kernel_index.shape[1], kernel_index.shape[2])
    me = lax.axis_index("coil").astype(jnp.int32)[None]
    temporal_all = gather_small(temporal, "frame")
    images = make_images(spatial, temporal_all)
    own = send_images(images)
    frames = own.shape[0]

    sig, dif, sig0, wide = prepare_call(kernel_index, kernel_level, sensitivity, perms, images)
    blocks = []
    coils = list(range(sensitivity.shape[0]))
    for frame in range(frames):
        parts = (gather_direct if frame else gather_blocks)(own[frame], "coil")
        groups = [coils[:1], coils[1:]] if frame and len(coils) > 1 else [coils]
        before = blocks[-1][:1] if blocks else []
        for group in groups:
            before = normal_call(frame, group, me, parts, wide, sig, dif, sig0, coil_data, tables, before)
        blocks.append(before)
    gradient = 0.0
    for frame in range(frames):
        final = frame == frames - 1
        rows_sum = (scatter_blocks if final else scatter_direct)(blocks[frame], "coil")
        residual = send_residual(rows_sum)
        gradient = gradient + jnp.einsum(
            "fr,fcxy->rcxy", temporal_all[:, frame], residual, precision=lax.Precision.HIGHEST
        )
    spatial_next = spatial - STEP_SIZE * gradient
    parts = gather_blocks(send_images(make_images(spatial_next, temporal_all)), "coil")
    return spatial_next, place_call(me, parts)


def solution(mesh):
    placed = (
        P(None, None, "coil", "frame"),
        P("frame", None),
        P("coil", None, None, None),
        P("frame", "coil", None, None, None),
        P("frame", None, None),
        P("frame", None),
    )
    return jax.shard_map(
        body,
        mesh=mesh,
        in_specs=placed,
        out_specs=(P(None, None, "coil", "frame"), P("frame", None, None, None)),
        check_vma=False,
    )
```

```python
import functools
import jax, jax.numpy as jnp, numpy as np
from jax import lax
from jax.sharding import PartitionSpec as P
from jax.experimental import pallas as pl
from jax.experimental.pallas import tpu as pltpu

STEP_SIZE = 0.15
LANES = 128
VMEM_BYTES = 67043328
F32, BF16 = jnp.float32, jnp.bfloat16


def halves(table):
    high = np.asarray(table, np.float32).astype(BF16)
    low = (table - high.astype(np.float64)).astype(np.float32).astype(BF16)
    return high, low


def wave(count, places, period):
    turns = np.outer(np.arange(count), places) % (2 * period)
    slot = np.outer([period // 2], places) % (2 * period)
    angle = np.pi / period * turns
    cosine, sine = np.cos(angle), np.sin(angle)
    sine[0] = np.sin(np.pi / period * slot[0])
    return cosine, sine


def row_tables(rows, period):
    cosine, sine = wave(rows, 2 * np.arange(rows // 2) + 1, period)
    forward, inverse = [], []
    for table in (cosine, sine):
        high, low = halves(table)
        forward.append(np.concatenate([high, high, low], 1))
        inverse.append(np.concatenate([high.T, high.T, low.T], 1))
    return np.stack(forward), np.stack(inverse)


def col_tables(cols, period):
    main = cols // LANES * LANES
    cosine, sine = wave(cols, 2 * np.arange(cols) - (cols - 1), period)
    mixed = np.concatenate([cosine[:main], sine[:main], cosine[main:], sine[main:]], 0).T
    high, low = halves(mixed)
    blank = np.zeros((cols - main, mixed.shape[1]), BF16)
    forward = np.concatenate([high[:main], high[:main], low[:main], high[main:], high[main:], low[main:], blank], 0)
    high, low = high.T, low.T
    inverse = np.concatenate([high, high, low], 0)
    return forward, inverse


def split(value):
    high = value.astype(BF16)
    return high, (value - high.astype(F32)).astype(BF16)


def dot(left, right):
    return jnp.dot(left, right, preferred_element_type=F32)


def packing(count, width):
    groups = LANES // width
    lines = -(-2 * count // groups)
    return groups, -(-lines // 8) * 8


def pack(rows, width):
    total, cols = rows.shape
    groups, lines = packing(total // 2, width)
    missing = groups * lines - total
    if missing:
        rows = jnp.concatenate([rows, jnp.zeros((missing, cols), rows.dtype)], 0)
    rest = LANES - groups * width
    packed = []
    for at in range(0, cols, width):
        pieces = [rows[g * lines : (g + 1) * lines, at : at + width] for g in range(groups)]
        if rest:
            pieces.append(jnp.zeros((lines, rest), rows.dtype))
        packed.append(jnp.concatenate(pieces, 1))
    return packed


def unpack(packed, total, width):
    groups, _ = packing(total // 2, width)
    bands = [jnp.concatenate([p[:, g * width : (g + 1) * width] for p in packed], 1) for g in range(groups)]
    return jnp.concatenate(bands, 0)[:total]


def normal_kernel(size, extra, frame, first_coil, me_ref, *refs):
    parts_hbm, refs = refs[:size], refs[size:]
    sens_hbm, sig_hbm, dif_hbm, data_hbm, tcol_hbm, trow_hbm, tback_hbm, tlast_hbm, sig0_ref, rev_ref = refs[:10]
    before, refs = refs[10 : 10 + extra], refs[10 + extra :]
    blocks, refs = refs[:size], refs[size:]
    sens_ref, tcol_ref, trow_ref, sig_ref, dif_ref, tback_ref, tlast_ref, data_ref, sems = refs[:9]
    parts, img_n, img_s, xcat, mid, back, last, acc = refs[9:]
    arrived = [pltpu.make_async_copy(parts_hbm[n].at[:, frame], parts.at[n], sems.at[8 + n]) for n in range(size)]
    for copy in arrived:
        copy.start()
    chosen = pl.ds(first_coil, sens_ref.shape[0])
    moved = [
        pltpu.make_async_copy(source, target, sems.at[n])
        for n, (source, target) in enumerate((
            (sens_hbm.at[chosen], sens_ref), (tcol_hbm, tcol_ref), (trow_hbm, trow_ref), (sig_hbm.at[frame], sig_ref), (dif_hbm.at[frame], dif_ref),
            (tback_hbm, tback_ref), (tlast_hbm, tlast_ref), (data_hbm.at[frame, chosen], data_ref),
        ))
    ]
    for copy in moved:
        copy.start()
    coils, _, rows, _ = sens_ref.shape
    cols = acc.shape[2]
    half = rows // 2
    main = cols // LANES * LANES
    spectral = tcol_ref.shape[1]
    steps = spectral // LANES
    count = rows // size

    def place(number):
        return pl.ds(pl.multiple_of((me_ref[0] ^ number) * count, count), count)

    width = cols // parts.shape[1]
    for number in range(size):
        arrived[number].wait()
        block = unpack([parts[number, n].astype(F32) for n in range(cols // width)], 2 * count, width)
        for part in range(2):
            img_n[part, place(number)] = block[part * count : (part + 1) * count].astype(BF16)
    for part in range(2):
        for top, value in enumerate((img_n[part, half:].astype(F32), dot(rev_ref[...], img_n[part, :half]))):
            here = slice(top * half, top * half + half)
            img_s[part, here, :main] = value[:, :main]
            img_s[part, here, main:] = jnp.concatenate([value[:, main:]] * (LANES // (cols - main)), 1)
    moved[0].wait()
    lane = lax.broadcasted_iota(jnp.int32, (half, LANES), 1)
    keep = (lane > 0).astype(F32)
    low_lane = lane < (cols - main)

    def one_coil(coil, carry):
        sums = {}
        for top in range(2):
            here = slice(top * half, top * half + half)
            s_re = sens_ref[coil, 0, here].astype(F32)
            s_im = sens_ref[coil, 1, here].astype(F32)
            i_re, i_im = img_s[0, here], img_s[1, here]
            sums[top, 0] = s_re * i_re - s_im * i_im
            sums[top, 1] = s_re * i_im + s_im * i_re
        for part in range(2):
            for sign in range(2):
                value = sums[0, part] + sums[1, part] if sign == 0 else sums[0, part] - sums[1, part]
                high, low = split(value)
                there = slice((2 * sign + part) * half, (2 * sign + part + 1) * half)
                xcat[there, :main] = high[:, :main]
                xcat[there, main : 2 * main] = low[:, :main]
                xcat[there, 2 * main : 2 * main + LANES] = jnp.where(low_lane, high[:, main:], low[:, main:])
                xcat[there, 2 * main + LANES :] = high[:, main:]

        @pl.when(coil == 0)
        def _():
            moved[1].wait()

        for sign in range(2):
            lines = slice(2 * sign * half, (2 * sign + 2) * half)
            spread = [xcat[lines, : 2 * main], xcat[lines, :main], xcat[lines, 2 * main :]]
            both = dot(jnp.concatenate(spread, 1), tcol_ref[...])
            re, im = both[:half], both[half:]
            for step in range(steps):
                at = step * LANES
                if at < main:
                    c_re, c_im = re[:, at : at + LANES], im[:, at : at + LANES]
                    s_re, s_im = re[:, main + at : main + at + LANES], im[:, main + at : main + at + LANES]
                    if at == 0:
                        s_re, s_im = s_re * keep, s_im * keep
                    m_re, m_im = c_re + s_im, c_im - s_re
                elif at < 2 * main:
                    c_re, c_im = re[:, at - main : at - main + LANES], im[:, at - main : at - main + LANES]
                    s_re, s_im = re[:, at : at + LANES], im[:, at : at + LANES]
                    if at == main:
                        c_re, c_im = c_re * keep, c_im * keep
                    m_re, m_im = c_re - s_im, c_im + s_re
                else:
                    g_re, g_im = re[:, at : at + LANES], im[:, at : at + LANES]
                    m_re = g_re + pltpu.roll(g_im, LANES // 2, 1)
                    m_im = g_im - pltpu.roll(g_re, LANES // 2, 1)
                for part, value in enumerate((m_re, m_im)):
                    high, low = split(value)
                    there = slice((2 * step + part) * LANES, (2 * step + part + 1) * LANES)
                    mid[sign, :half, there] = high
                    mid[sign, half:, there] = low

        @pl.when(coil == 0)
        def _():
            for copy in moved[2:6]:
                copy.wait()

        def one_step(step, carry):
            there = pl.ds(pl.multiple_of(step * 2 * LANES, 2 * LANES), 2 * LANES)
            here = pl.ds(pl.multiple_of(step * LANES, LANES), LANES)
            even, odd = [
                dot(trow_ref[sign], jnp.concatenate([mid[sign, :, there], mid[sign, :half, there]], 0)) for sign in range(2)
            ]
            sig, dif = sig_ref[:, here], dif_ref[:, here]
            c_re, c_im = even[:, :LANES], even[:, LANES:]
            s_re, s_im = odd[:, :LANES], odd[:, LANES:]
            p_re = sig * c_re + dif * s_im
            p_im = sig * c_im - dif * s_re
            q_re = sig * s_re - dif * c_im
            q_im = sig * s_im + dif * c_re
            first = sig0_ref[frame, :, here]
            q_re = jnp.concatenate([first * s_re[:8] - dif[:8] * c_im[:8], q_re[8:]], 0)
            q_im = jnp.concatenate([first * s_im[:8] + dif[:8] * c_re[:8], q_im[8:]], 0)
            for number, pair in enumerate(((p_re, p_im), (q_re, q_im))):
                both = [split(value) for value in pair]
                high, low = [jnp.concatenate([both[0][n], both[1][n]], 1) for n in range(2)]
                back[number, :, there] = dot(tback_ref[number], jnp.concatenate([high, low, high], 0))
            return carry

        lax.fori_loop(0, steps, one_step, 0, unroll=True)
        for sign in range(2):
            for step in range(steps):
                at = step * LANES

                def piece(index, part):
                    return back[sign, :, (2 * index + part) * LANES : (2 * index + part + 1) * LANES]

                shift = main // LANES
                if at < main:
                    u_re, u_im = piece(step, 0), piece(step, 1)
                    v_re, v_im = piece(step + shift, 0), piece(step + shift, 1)
                    if at == 0:
                        v_re, v_im = v_re * keep, v_im * keep
                    w_re, w_im = u_re + v_re, u_im + v_im
                elif at < 2 * main:
                    u_re, u_im = piece(step - shift, 0), piece(step - shift, 1)
                    v_re, v_im = piece(step, 0), piece(step, 1)
                    if at == main:
                        u_re, u_im = u_re * keep, u_im * keep
                    w_re, w_im = v_im - u_im, u_re - v_re
                else:
                    g_re, g_im = piece(step, 0), piece(step, 1)
                    w_re = g_re - pltpu.roll(g_im, LANES // 2, 1)
                    w_im = g_im + pltpu.roll(g_re, LANES // 2, 1)
                for part, value in enumerate((w_re, w_im)):
                    high, low = split(value)
                    there = slice((2 * sign + part) * half, (2 * sign + part + 1) * half)
                    last[there, at : at + LANES] = high
                    last[there, spectral + at : spectral + at + LANES] = low

        @pl.when(coil == 0)
        def _():
            moved[6].wait()
            moved[7].wait()

        final = dot(jnp.concatenate([last[...], last[:, :spectral]], 1), tlast_ref[...])
        plus_re, plus_im, minus_re, minus_im = [final[n * half : (n + 1) * half] for n in range(4)]
        for top in range(2):
            here = slice(top * half, top * half + half)
            n_re = plus_re + minus_re if top == 0 else plus_re - minus_re
            n_im = plus_im + minus_im if top == 0 else plus_im - minus_im
            if top == 0:
                d_re, d_im = data_ref[coil, 0, half:].astype(F32), data_ref[coil, 1, half:].astype(F32)
            else:
                d_re, d_im = dot(rev_ref[...], data_ref[coil, 0, :half]), dot(rev_ref[...], data_ref[coil, 1, :half])
            n_re, n_im = n_re - d_re, n_im - d_im
            s_re = sens_ref[coil, 0, here, :cols].astype(F32)
            s_im = sens_ref[coil, 1, here, :cols].astype(F32)
            acc[0, here] += s_re * n_re + s_im * n_im
            acc[1, here] += s_re * n_im - s_im * n_re
        return carry

    acc[...] = jnp.zeros_like(acc)
    lax.fori_loop(0, coils, one_coil, 0)
    for part in range(2):
        above, below = acc[part, :half], acc[part, half:]
        high, low = split(below)
        rest = (below - high.astype(F32) - low.astype(F32)).astype(BF16)
        turned = dot(rev_ref[...], high) + dot(rev_ref[...], low) + dot(rev_ref[...], rest)
        acc[part, half:] = above
        acc[part, :half] = turned
    for number in range(size):
        block = jnp.concatenate([acc[part, place(number)] for part in range(2)], 0)
        for n, value in enumerate(pack(block, width)):
            blocks[number][n] = value + before[number][n] if extra == size else value


def normal_call(frame, chosen, me, parts, sens, sig, dif, sig0, data, tables, before):
    size = len(parts)
    rows, wide = sens.shape[2:]
    coils = len(chosen)
    cols = data.shape[4]
    half = rows // 2
    tcol, tlast, trow, tback, rev = tables
    spectral = tcol.shape[1]
    held = pl.BlockSpec(memory_space=pltpu.VMEM)
    away = pl.BlockSpec(memory_space=pl.ANY)
    like = lambda value: pltpu.VMEM(value.shape, value.dtype)
    one = lambda value: pltpu.VMEM(value.shape[1:], value.dtype)
    some = lambda value: pltpu.VMEM((coils,) + value.shape[1:], value.dtype)
    packed = parts[0].shape[:1] + parts[0].shape[2:]
    flops = 2 * coils * 2 * 12 * rows * cols * spectral

    return pl.pallas_call(
        functools.partial(normal_kernel, size, len(before), frame, chosen[0]),
        out_shape=[jax.ShapeDtypeStruct(packed, F32)] * size,
        in_specs=[pl.BlockSpec(memory_space=pltpu.SMEM)] + [away] * (size + 8) + [held] * 2 + [held if len(before) == size else away] * len(before),
        out_specs=[held] * size,
        scratch_shapes=[
            some(sens), like(tcol), like(trow), one(sig), one(dif), like(tback), like(tlast), some(one(data)),
            pltpu.SemaphoreType.DMA((8 + size,)),
            pltpu.VMEM((size,) + packed, BF16),
            pltpu.VMEM((2, rows, cols), BF16),
            pltpu.VMEM((2, rows, wide), F32),
            pltpu.VMEM((4 * half, tcol.shape[0] * 3 // 4), BF16),
            pltpu.VMEM((2, 2 * half, 2 * spectral), BF16),
            pltpu.VMEM((2, half, 2 * spectral), F32),
            pltpu.VMEM((4 * half, 2 * spectral), BF16),
            pltpu.VMEM((2, rows, cols), F32),
        ],
        compiler_params=pltpu.CompilerParams(vmem_limit_bytes=VMEM_BYTES),
        cost_estimate=pl.CostEstimate(flops=flops, bytes_accessed=8 * 1024 * 1024, transcendentals=0),
    )(me, *parts, sens, sig, dif, data, tcol, trow, tback, tlast, sig0, rev, *before)


def place_kernel(numbers, extra, me_ref, *refs):
    total = len(numbers)
    parts_hbm, out_hbm = refs[:total], refs[total + extra]
    parts, blocks, sems = refs[total + extra + 1 :]
    _, devices, frames, _, _ = parts.shape
    count = blocks.shape[3]
    width = blocks.shape[4] // devices
    arrived = [pltpu.make_async_copy(parts_hbm[n], parts.at[n], sems.at[n]) for n in range(total)]
    for copy in arrived:
        copy.start()
    leaving = []
    for n, number in enumerate(numbers):
        arrived[n].wait()
        for frame in range(frames):
            block = unpack([parts[n, device, frame].astype(F32) for device in range(devices)], 2 * count, width)
            for part in range(2):
                blocks[n, frame, part] = block[part * count : (part + 1) * count].astype(BF16)
        there = pl.ds(pl.multiple_of((me_ref[0] ^ number) * count, count), count)
        leaving.append(pltpu.make_async_copy(blocks.at[n], out_hbm.at[:, :, there], sems.at[total + n]))
        leaving[-1].start()
    for copy in leaving:
        copy.wait()


def place_call(me, parts, size, count, width, before):
    numbers = sorted(parts)
    devices, frames = parts[numbers[0]].shape[:2]
    away = pl.BlockSpec(memory_space=pl.ANY)
    total = len(numbers)
    return pl.pallas_call(
        functools.partial(place_kernel, numbers, len(before)),
        out_shape=jax.ShapeDtypeStruct((frames, 2, count * size, width * devices), BF16),
        in_specs=[pl.BlockSpec(memory_space=pltpu.SMEM)] + [away] * (total + len(before)),
        out_specs=away,
        input_output_aliases={1 + total: 0} if before else {},
        scratch_shapes=[
            pltpu.VMEM((total,) + parts[numbers[0]].shape, BF16),
            pltpu.VMEM((total, frames, 2, count, width * devices), BF16),
            pltpu.SemaphoreType.DMA((2 * total,)),
        ],
        compiler_params=pltpu.CompilerParams(vmem_limit_bytes=VMEM_BYTES),
        cost_estimate=pl.CostEstimate(flops=1 << 20, bytes_accessed=4 * 1024 * 1024, transcendentals=0),
    )(me, *[parts[number] for number in numbers], *before)


def pack_kernel(factor_ref, out_ref):
    for rank in range(factor_ref.shape[0]):
        rows = jnp.concatenate([factor_ref[rank, 0].T, factor_ref[rank, 1].T], 0)
        out_ref[rank] = pack(rows, factor_ref.shape[2])[0]


def pack_call(factors):
    ranks, _, count, width = factors.shape
    lines = packing(count, width)[1]
    shape = jax.ShapeDtypeStruct((ranks, lines, LANES), F32)
    return pl.pallas_call(pack_kernel, out_shape=shape)(factors.transpose(0, 1, 3, 2))


def unpack_kernel(packed_ref, out_ref):
    _, _, width, count = out_ref.shape
    for rank in range(out_ref.shape[0]):
        block = unpack([packed_ref[rank]], 2 * count, width)
        out_ref[rank, 0], out_ref[rank, 1] = block[:count].T, block[count:].T


def unpack_call(packed, shape):
    turned = jax.ShapeDtypeStruct(shape[:2] + (shape[3], shape[2]), F32)
    return pl.pallas_call(unpack_kernel, out_shape=turned)(packed).transpose(0, 1, 3, 2)


def mix(temporal_ref, factors, images_ref):
    devices, frames, ranks = temporal_ref.shape
    for device in range(devices):
        for frame in range(frames):
            value = temporal_ref[device, frame, 0] * factors[0]
            for rank in range(1, ranks):
                value = value + temporal_ref[device, frame, rank] * factors[rank]
            images_ref[device, frame] = value.astype(BF16)


def images_kernel(temporal_ref, factor_ref, images_ref):
    mix(temporal_ref, [factor_ref[rank] for rank in range(factor_ref.shape[0])], images_ref)


def update_kernel(temporal_ref, factor_ref, residual_ref, next_ref, images_ref):
    devices, frames, ranks = temporal_ref.shape
    factors = []
    for rank in range(ranks):
        gradient = 0.0
        for frame in range(frames):
            for device in range(devices):
                gradient = gradient + temporal_ref[device, frame, rank] * residual_ref[device, frame]
        factors.append(factor_ref[rank] - STEP_SIZE * gradient)
        next_ref[rank] = factors[rank]
    mix(temporal_ref, factors, images_ref)


def images_call(temporal_all, packed):
    devices, frames, _ = temporal_all.shape
    return pl.pallas_call(
        images_kernel,
        out_shape=jax.ShapeDtypeStruct((devices, frames) + packed.shape[1:], BF16),
        in_specs=[pl.BlockSpec(memory_space=pltpu.SMEM), pl.BlockSpec(memory_space=pltpu.VMEM)],
    )(temporal_all, packed)


def update_call(temporal_all, packed, residual):
    devices, frames, _ = temporal_all.shape
    held = pl.BlockSpec(memory_space=pltpu.VMEM)
    return pl.pallas_call(
        update_kernel,
        out_shape=(
            jax.ShapeDtypeStruct(packed.shape, F32),
            jax.ShapeDtypeStruct((devices, frames) + packed.shape[1:], BF16),
        ),
        in_specs=[pl.BlockSpec(memory_space=pltpu.SMEM)] + [held] * 2,
    )(temporal_all, packed, residual)


def freq_order_rows(rows, period):
    k = np.arange(rows)
    return np.concatenate([k, np.where(k == 0, period // 2, period - k)])


def freq_order_cols(cols, period):
    main = cols // LANES * LANES
    l = np.arange(cols)
    u, v = l, np.where(l == 0, period // 2, period - l)
    return np.concatenate([u[:main], v[:main], u[main:], v[main:]])


def prepare_kernel(index_ref, level_ref, sens_ref, row_ref, col_ref, rev_ref, dup_ref, after_ref, sig_ref, dif_ref, sig0_ref, out_ref):
    frame = pl.program_id(0)
    rows = sig_ref.shape[1]
    half = rows // 2
    levels = level_ref.shape[1]
    scale = 1.0 / (index_ref.shape[1] * index_ref.shape[2])

    def values(index):
        place = dot(index, col_ref[...])
        kernel = jnp.full(place.shape, level_ref[frame, 0] * scale, F32)
        for number in range(1, levels):
            kernel = jnp.where(place > number - 0.5, level_ref[frame, number] * scale, kernel)
        return kernel

    upper = values(index_ref[0, :rows].astype(F32).astype(BF16))
    turned = dot(row_ref[...], index_ref[0, rows:].astype(F32).astype(BF16))
    lower = values(turned.astype(BF16))
    first = lax.broadcasted_iota(jnp.int32, upper[:8].shape, 0) == 0
    sig_ref[0] = upper + lower
    dif_ref[0] = upper - lower
    sig_ref[0, :8] = jnp.where(first, upper[:8], upper[:8] + lower[:8])
    sig0_ref[0] = jnp.where(first, lower[:8], upper[:8] + lower[:8])
    dif_ref[0, :8] = jnp.where(first, 0.0, upper[:8] - lower[:8])

    for part in range(2):
        wide = dot(sens_ref[0, part], dup_ref[...]).astype(BF16)
        out_ref[0, part, :half] = wide[half:]
        out_ref[0, part, half:] = dot(rev_ref[...], wide[:half]).astype(BF16)


def prepare_call(index, level, sens, perms, after):
    frames, rows_pad, cols_pad = index.shape
    coils, _, rows, cols = sens.shape
    row, col, rev, dup = perms
    whole = lambda n: (lambda f: (0,) * n)
    block = lambda *shape: pl.BlockSpec((1,) + shape, lambda f: (f,) + (0,) * len(shape))
    return pl.pallas_call(
        prepare_kernel,
        grid=(frames,),
        out_shape=(
            jax.ShapeDtypeStruct((frames, rows, cols_pad), F32),
            jax.ShapeDtypeStruct((frames, rows, cols_pad), F32),
            jax.ShapeDtypeStruct((frames, 8, cols_pad), F32),
            jax.ShapeDtypeStruct((coils, 2, rows, dup.shape[1]), BF16),
        ),
        in_specs=[
            block(rows_pad, cols_pad),
            pl.BlockSpec(memory_space=pltpu.SMEM),
            block(2, rows, cols),
            pl.BlockSpec(row.shape, whole(2)),
            pl.BlockSpec(col.shape, whole(2)),
            pl.BlockSpec(rev.shape, whole(2)),
            pl.BlockSpec(dup.shape, whole(2)),
            pl.BlockSpec(memory_space=pl.ANY),
        ],
        out_specs=(block(rows, cols_pad), block(rows, cols_pad), block(8, cols_pad), block(2, rows, dup.shape[1])),
        compiler_params=pltpu.CompilerParams(vmem_limit_bytes=VMEM_BYTES),
        cost_estimate=pl.CostEstimate(flops=6 * frames * rows * cols_pad * cols_pad, bytes_accessed=16 * 1024 * 1024, transcendentals=0),
    )(index, level, sens, row, col, rev, dup, after)


def one_hot(order):
    return (order[:, None] == np.arange(len(order))[None, :]).astype(BF16)


def constants(rows, cols, rows_pad, cols_pad):
    assert rows_pad == 2 * rows and cols_pad == 2 * cols
    main = cols // LANES * LANES
    assert 2 * (cols - main) == LANES and rows % 32 == 0
    forward, inverse = row_tables(rows, rows_pad)
    first, last = col_tables(cols, cols_pad)
    turn = np.arange(rows // 2)[::-1]
    flip = freq_order_rows(rows, rows_pad)[rows:] - rows
    spread = np.concatenate([np.arange(cols), np.arange(main, cols)])
    rev, row = one_hot(turn), one_hot(flip)
    col = one_hot(freq_order_cols(cols, cols_pad)).T
    dup = (np.arange(cols)[:, None] == spread[None, :]).astype(BF16)
    tables = [jnp.asarray(t) for t in (first, last, forward, inverse, rev)]
    return tables, [jnp.asarray(t) for t in (row, col, rev, dup)]


def exchange(value, axis, distance):
    size = lax.axis_size(axis)
    return lax.ppermute(value, axis, [(i, i ^ distance) for i in range(size)])


def gather_blocks(own, axis):
    held = {0: own}
    distance = lax.axis_size(axis) // 2
    while distance:
        for key in list(held):
            held[key ^ distance] = exchange(held[key], axis, distance)
        distance //= 2
    return held


def scatter_blocks(blocks, axis):
    held = dict(enumerate(blocks))
    distance = 1
    while distance < lax.axis_size(axis):
        held = {
            key: value + exchange(held[key ^ distance], axis, distance)
            for key, value in held.items()
            if not key & distance
        }
        distance *= 2
    return held[0]


def scatter_direct(blocks, axis):
    total = blocks[0]
    for distance in range(1, lax.axis_size(axis)):
        total = total + exchange(blocks[distance], axis, distance)
    return total


def gather_small(value, axis):
    size = lax.axis_size(axis)
    me = lax.axis_index(axis)
    held = value[None]
    distance = 1
    while distance < size:
        other = exchange(held, axis, distance)
        upper = (me // distance) % 2 == 1
        held = jnp.where(upper, jnp.concatenate([other, held]), jnp.concatenate([held, other]))
        distance *= 2
    return held


def swap(value):
    return lax.all_to_all(value, "frame", split_axis=0, concat_axis=0, tiled=True)


def body(spatial, temporal, sensitivity, coil_data, kernel_index, kernel_level):
    rows, cols = sensitivity.shape[2:]
    tables, perms = constants(rows, cols, kernel_index.shape[1], kernel_index.shape[2])
    me = lax.axis_index("coil").astype(jnp.int32)[None]
    size = lax.axis_size("coil")
    temporal_all = gather_small(temporal, "frame")
    packed = pack_call(spatial)
    images = images_call(temporal_all, packed)
    own = swap(images)
    frames = own.shape[1]

    sig, dif, sig0, wide = prepare_call(kernel_index, kernel_level, sensitivity, perms, images)
    held = gather_blocks(own, "coil")
    parts = [held[number] for number in range(size)]
    blocks = []
    coils = range(sensitivity.shape[0])
    for frame in range(frames):
        before = blocks[-1][:1] if blocks else []
        blocks.append(normal_call(frame, coils, me, parts, wide, sig, dif, sig0, coil_data, tables, before))
    sums = []
    for frame in range(frames):
        sums.append((scatter_blocks if frame == frames - 1 else scatter_direct)(blocks[frame], "coil"))
    residual = swap(jnp.stack(sums, 1))
    packed_next, images = update_call(temporal_all, packed, residual)
    own = swap(images)
    spatial_next = unpack_call(packed_next, spatial.shape)
    held = gather_blocks(own, "coil")
    out = []
    for chosen in (range(size // 2), range(size // 2, size)):
        group = {number: held[number] for number in chosen}
        out = [place_call(me, group, size, spatial.shape[2], spatial.shape[3], out)]
    return spatial_next, out[0]


def solution(mesh):
    placed = (
        P(None, None, "coil", "frame"),
        P("frame", None),
        P("coil", None, None, None),
        P("frame", "coil", None, None, None),
        P("frame", None, None),
        P("frame", None),
    )
    return jax.shard_map(
        body,
        mesh=mesh,
        in_specs=placed,
        out_specs=(P(None, None, "coil", "frame"), P("frame", None, None, None)),
        check_vma=False,
    )
```

```python
import functools
import jax, jax.numpy as jnp, numpy as np
from jax import lax
from jax.sharding import PartitionSpec as P
from jax.experimental import pallas as pl
from jax.experimental.pallas import tpu as pltpu

STEP_SIZE = 0.15
LANES = 128
VMEM_BYTES = 67043328
F32, BF16 = jnp.float32, jnp.bfloat16


def halves(table):
    high = np.asarray(table, np.float32).astype(BF16)
    low = (table - high.astype(np.float64)).astype(np.float32).astype(BF16)
    return high, low


def wave(count, places, period):
    turns = np.outer(np.arange(count), places) % (2 * period)
    slot = np.outer([period // 2], places) % (2 * period)
    angle = np.pi / period * turns
    cosine, sine = np.cos(angle), np.sin(angle)
    sine[0] = np.sin(np.pi / period * slot[0])
    return cosine, sine


def row_tables(rows, period):
    cosine, sine = wave(rows, 2 * np.arange(rows // 2) + 1, period)
    forward, inverse = [], []
    for table in (cosine, sine):
        high, low = halves(table)
        forward.append(np.concatenate([high, high, low], 1))
        inverse.append(np.concatenate([high.T, high.T, low.T], 1))
    return np.stack(forward), np.stack(inverse)


def col_tables(cols, period):
    main = cols // LANES * LANES
    cosine, sine = wave(cols, 2 * np.arange(cols) - (cols - 1), period)
    mixed = np.concatenate([cosine[:main], sine[:main], cosine[main:], sine[main:]], 0).T
    high, low = halves(mixed)
    blank = np.zeros((cols - main, mixed.shape[1]), BF16)
    forward = np.concatenate([high[:main], high[:main], low[:main], high[main:], high[main:], low[main:], blank], 0)
    high, low = high.T, low.T
    inverse = np.concatenate([high, high, low], 0)
    return forward, inverse


def split(value):
    high = value.astype(BF16)
    return high, (value - high.astype(F32)).astype(BF16)


def dot(left, right):
    return jnp.dot(left, right, preferred_element_type=F32)


def packing(count, width):
    groups = LANES // width
    lines = -(-2 * count // groups)
    return groups, -(-lines // 8) * 8


def pack(rows, width):
    total, cols = rows.shape
    groups, lines = packing(total // 2, width)
    missing = groups * lines - total
    if missing:
        rows = jnp.concatenate([rows, jnp.zeros((missing, cols), rows.dtype)], 0)
    rest = LANES - groups * width
    packed = []
    for at in range(0, cols, width):
        pieces = [rows[g * lines : (g + 1) * lines, at : at + width] for g in range(groups)]
        if rest:
            pieces.append(jnp.zeros((lines, rest), rows.dtype))
        packed.append(jnp.concatenate(pieces, 1))
    return packed


def unpack(packed, total, width):
    groups, _ = packing(total // 2, width)
    bands = [jnp.concatenate([p[:, g * width : (g + 1) * width] for p in packed], 1) for g in range(groups)]
    return jnp.concatenate(bands, 0)[:total]


def normal_kernel(size, extra, frame, first_coil, me_ref, *refs):
    parts_hbm, refs = refs[:size], refs[size:]
    sens_hbm, sig_hbm, dif_hbm, data_hbm, tcol_hbm, trow_hbm, tback_hbm, tlast_hbm, sig0_ref, rev_ref = refs[:10]
    before, refs = refs[10 : 10 + extra], refs[10 + extra :]
    blocks, refs = refs[:size], refs[size:]
    sens_ref, tcol_ref, trow_ref, sig_ref, dif_ref, tback_ref, tlast_ref, data_ref, sems = refs[:9]
    parts, img_n, img_s, xcat, mid, back, last, acc = refs[9:]
    arrived = [pltpu.make_async_copy(parts_hbm[n].at[:, frame], parts.at[n], sems.at[8 + n]) for n in range(size)]
    for copy in arrived:
        copy.start()
    chosen = pl.ds(first_coil, sens_ref.shape[0])
    moved = [
        pltpu.make_async_copy(source, target, sems.at[n])
        for n, (source, target) in enumerate((
            (sens_hbm.at[chosen], sens_ref), (tcol_hbm, tcol_ref), (trow_hbm, trow_ref), (sig_hbm.at[frame], sig_ref), (dif_hbm.at[frame], dif_ref),
            (tback_hbm, tback_ref), (tlast_hbm, tlast_ref), (data_hbm.at[frame, chosen], data_ref),
        ))
    ]
    for copy in moved:
        copy.start()
    coils, _, rows, _ = sens_ref.shape
    cols = acc.shape[2]
    half = rows // 2
    main = cols // LANES * LANES
    spectral = tcol_ref.shape[1]
    steps = spectral // LANES
    count = rows // size

    def place(number):
        return pl.ds(pl.multiple_of((me_ref[0] ^ number) * count, count), count)

    width = cols // parts.shape[1]
    for number in range(size):
        arrived[number].wait()
        block = unpack([parts[number, n].astype(F32) for n in range(cols // width)], 2 * count, width)
        for part in range(2):
            img_n[part, place(number)] = block[part * count : (part + 1) * count].astype(BF16)
    for part in range(2):
        for top, value in enumerate((img_n[part, half:].astype(F32), dot(rev_ref[...], img_n[part, :half]))):
            here = slice(top * half, top * half + half)
            img_s[part, here, :main] = value[:, :main]
            img_s[part, here, main:] = jnp.concatenate([value[:, main:]] * (LANES // (cols - main)), 1)
    moved[0].wait()
    lane = lax.broadcasted_iota(jnp.int32, (half, LANES), 1)
    keep = (lane > 0).astype(F32)
    low_lane = lane < (cols - main)

    def fold(coil):
        sums = {}
        for top in range(2):
            here = slice(top * half, top * half + half)
            s_re = sens_ref[coil, 0, here].astype(F32)
            s_im = sens_ref[coil, 1, here].astype(F32)
            i_re, i_im = img_s[0, here], img_s[1, here]
            sums[top, 0] = s_re * i_re - s_im * i_im
            sums[top, 1] = s_re * i_im + s_im * i_re
        for part in range(2):
            for sign in range(2):
                value = sums[0, part] + sums[1, part] if sign == 0 else sums[0, part] - sums[1, part]
                high, low = split(value)
                there = slice((2 * sign + part) * half, (2 * sign + part + 1) * half)
                xcat[coil, there, :main] = high[:, :main]
                xcat[coil, there, main : 2 * main] = low[:, :main]
                xcat[coil, there, 2 * main : 2 * main + LANES] = jnp.where(low_lane, high[:, main:], low[:, main:])
                xcat[coil, there, 2 * main + LANES :] = high[:, main:]

    def columns(coil):
        products = []
        for sign in range(2):
            lines = slice(2 * sign * half, (2 * sign + 2) * half)
            spread = [xcat[coil, lines, : 2 * main], xcat[coil, lines, :main], xcat[coil, lines, 2 * main :]]
            products.append(dot(jnp.concatenate(spread, 1), tcol_ref[...]))
        return products

    def mix_columns(coil, products):
        for sign in range(2):
            both = products[sign]
            re, im = both[:half], both[half:]
            for step in range(steps):
                at = step * LANES
                if at < main:
                    c_re, c_im = re[:, at : at + LANES], im[:, at : at + LANES]
                    s_re, s_im = re[:, main + at : main + at + LANES], im[:, main + at : main + at + LANES]
                    if at == 0:
                        s_re, s_im = s_re * keep, s_im * keep
                    m_re, m_im = c_re + s_im, c_im - s_re
                elif at < 2 * main:
                    c_re, c_im = re[:, at - main : at - main + LANES], im[:, at - main : at - main + LANES]
                    s_re, s_im = re[:, at : at + LANES], im[:, at : at + LANES]
                    if at == main:
                        c_re, c_im = c_re * keep, c_im * keep
                    m_re, m_im = c_re - s_im, c_im + s_re
                else:
                    g_re, g_im = re[:, at : at + LANES], im[:, at : at + LANES]
                    m_re = g_re + pltpu.roll(g_im, LANES // 2, 1)
                    m_im = g_im - pltpu.roll(g_re, LANES // 2, 1)
                for part, value in enumerate((m_re, m_im)):
                    high, low = split(value)
                    there = slice((2 * step + part) * LANES, (2 * step + part + 1) * LANES)
                    mid[coil, sign, :half, there] = high
                    mid[coil, sign, half:, there] = low


    def rows_pass(coil):
        def forward(step):
            there = slice(step * 2 * LANES, (step + 1) * 2 * LANES)
            return [
                dot(trow_ref[sign], jnp.concatenate([mid[coil, sign, :, there], mid[coil, sign, :half, there]], 0)) for sign in range(2)
            ]

        following = forward(0)
        for step in range(steps):
            there = slice(step * 2 * LANES, (step + 1) * 2 * LANES)
            here = slice(step * LANES, (step + 1) * LANES)
            even, odd = following
            if step + 1 < steps:
                following = forward(step + 1)
            sig, dif = sig_ref[:, here], dif_ref[:, here]
            c_re, c_im = even[:, :LANES], even[:, LANES:]
            s_re, s_im = odd[:, :LANES], odd[:, LANES:]
            p_re = sig * c_re + dif * s_im
            p_im = sig * c_im - dif * s_re
            q_re = sig * s_re - dif * c_im
            q_im = sig * s_im + dif * c_re
            first = sig0_ref[frame, :, here]
            q_re = jnp.concatenate([first * s_re[:8] - dif[:8] * c_im[:8], q_re[8:]], 0)
            q_im = jnp.concatenate([first * s_im[:8] + dif[:8] * c_re[:8], q_im[8:]], 0)
            for number, pair in enumerate(((p_re, p_im), (q_re, q_im))):
                both = [split(value) for value in pair]
                high, low = [jnp.concatenate([both[0][n], both[1][n]], 1) for n in range(2)]
                back[coil, number, :, there] = dot(tback_ref[number], jnp.concatenate([high, low, high], 0))

    def unmix_columns(coil):
        for sign in range(2):
            for step in range(steps):
                at = step * LANES

                def piece(index, part):
                    return back[coil, sign, :, (2 * index + part) * LANES : (2 * index + part + 1) * LANES]

                shift = main // LANES
                if at < main:
                    u_re, u_im = piece(step, 0), piece(step, 1)
                    v_re, v_im = piece(step + shift, 0), piece(step + shift, 1)
                    if at == 0:
                        v_re, v_im = v_re * keep, v_im * keep
                    w_re, w_im = u_re + v_re, u_im + v_im
                elif at < 2 * main:
                    u_re, u_im = piece(step - shift, 0), piece(step - shift, 1)
                    v_re, v_im = piece(step, 0), piece(step, 1)
                    if at == main:
                        u_re, u_im = u_re * keep, u_im * keep
                    w_re, w_im = v_im - u_im, u_re - v_re
                else:
                    g_re, g_im = piece(step, 0), piece(step, 1)
                    w_re = g_re - pltpu.roll(g_im, LANES // 2, 1)
                    w_im = g_im + pltpu.roll(g_re, LANES // 2, 1)
                for part, value in enumerate((w_re, w_im)):
                    high, low = split(value)
                    there = slice((2 * sign + part) * half, (2 * sign + part + 1) * half)
                    last[coil, there, at : at + LANES] = high
                    last[coil, there, spectral + at : spectral + at + LANES] = low

    def last_columns(coil):
        return dot(jnp.concatenate([last[coil], last[coil, :, :spectral]], 1), tlast_ref[...])

    def add_residual(coil, final):
        plus_re, plus_im, minus_re, minus_im = [final[n * half : (n + 1) * half] for n in range(4)]
        for top in range(2):
            here = slice(top * half, top * half + half)
            n_re = plus_re + minus_re if top == 0 else plus_re - minus_re
            n_im = plus_im + minus_im if top == 0 else plus_im - minus_im
            if top == 0:
                d_re, d_im = data_ref[coil, 0, half:].astype(F32), data_ref[coil, 1, half:].astype(F32)
            else:
                d_re, d_im = dot(rev_ref[...], data_ref[coil, 0, :half]), dot(rev_ref[...], data_ref[coil, 1, :half])
            n_re, n_im = n_re - d_re, n_im - d_im
            s_re = sens_ref[coil, 0, here, :cols].astype(F32)
            s_im = sens_ref[coil, 1, here, :cols].astype(F32)
            acc[0, here] += s_re * n_re + s_im * n_im
            acc[1, here] += s_re * n_im - s_im * n_re

    acc[...] = jnp.zeros_like(acc)
    fold(0)
    moved[1].wait()
    products = columns(0)
    for coil in range(coils):
        if coil + 1 < coils:
            fold(coil + 1)
        mix_columns(coil, products)
        if coil == 0:
            for copy in moved[2:6]:
                copy.wait()
        rows_pass(coil)
        if coil + 1 < coils:
            products = columns(coil + 1)
        unmix_columns(coil)
        if coil == 0:
            moved[6].wait()
            moved[7].wait()
        add_residual(coil, last_columns(coil))
    for part in range(2):
        above, below = acc[part, :half], acc[part, half:]
        high, low = split(below)
        rest = (below - high.astype(F32) - low.astype(F32)).astype(BF16)
        turned = dot(rev_ref[...], high) + dot(rev_ref[...], low) + dot(rev_ref[...], rest)
        acc[part, half:] = above
        acc[part, :half] = turned
    for number in range(size):
        block = jnp.concatenate([acc[part, place(number)] for part in range(2)], 0)
        for n, value in enumerate(pack(block, width)):
            blocks[number][n] = value + before[number][n] if extra == size else value


def normal_call(frame, chosen, me, parts, sens, sig, dif, sig0, data, tables, before):
    size = len(parts)
    rows, wide = sens.shape[2:]
    coils = len(chosen)
    cols = data.shape[4]
    half = rows // 2
    tcol, tlast, trow, tback, rev = tables
    spectral = tcol.shape[1]
    held = pl.BlockSpec(memory_space=pltpu.VMEM)
    away = pl.BlockSpec(memory_space=pl.ANY)
    like = lambda value: pltpu.VMEM(value.shape, value.dtype)
    one = lambda value: pltpu.VMEM(value.shape[1:], value.dtype)
    some = lambda value: pltpu.VMEM((coils,) + value.shape[1:], value.dtype)
    packed = parts[0].shape[:1] + parts[0].shape[2:]
    flops = 2 * coils * 2 * 12 * rows * cols * spectral

    return pl.pallas_call(
        functools.partial(normal_kernel, size, len(before), frame, chosen[0]),
        out_shape=[jax.ShapeDtypeStruct(packed, F32)] * size,
        in_specs=[pl.BlockSpec(memory_space=pltpu.SMEM)] + [away] * (size + 8) + [held] * 2 + [held if len(before) == size else away] * len(before),
        out_specs=[held] * size,
        scratch_shapes=[
            some(sens), like(tcol), like(trow), one(sig), one(dif), like(tback), like(tlast), some(one(data)),
            pltpu.SemaphoreType.DMA((8 + size,)),
            pltpu.VMEM((size,) + packed, BF16),
            pltpu.VMEM((2, rows, cols), BF16),
            pltpu.VMEM((2, rows, wide), F32),
            pltpu.VMEM((coils, 4 * half, tcol.shape[0] * 3 // 4), BF16),
            pltpu.VMEM((coils, 2, 2 * half, 2 * spectral), BF16),
            pltpu.VMEM((coils, 2, half, 2 * spectral), F32),
            pltpu.VMEM((coils, 4 * half, 2 * spectral), BF16),
            pltpu.VMEM((2, rows, cols), F32),
        ],
        compiler_params=pltpu.CompilerParams(vmem_limit_bytes=VMEM_BYTES - (1 << 20)),
        cost_estimate=pl.CostEstimate(flops=flops, bytes_accessed=8 * 1024 * 1024, transcendentals=0),
    )(me, *parts, sens, sig, dif, data, tcol, trow, tback, tlast, sig0, rev, *before)


def place_kernel(numbers, extra, me_ref, *refs):
    total = len(numbers)
    parts_hbm, out_hbm = refs[:total], refs[total + extra]
    parts, blocks, sems = refs[total + extra + 1 :]
    _, devices, frames, _, _ = parts.shape
    count = blocks.shape[3]
    width = blocks.shape[4] // devices
    arrived = [pltpu.make_async_copy(parts_hbm[n], parts.at[n], sems.at[n]) for n in range(total)]
    for copy in arrived:
        copy.start()
    leaving = []
    for n, number in enumerate(numbers):
        arrived[n].wait()
        for frame in range(frames):
            block = unpack([parts[n, device, frame].astype(F32) for device in range(devices)], 2 * count, width)
            for part in range(2):
                blocks[n, frame, part] = block[part * count : (part + 1) * count].astype(BF16)
        there = pl.ds(pl.multiple_of((me_ref[0] ^ number) * count, count), count)
        leaving.append(pltpu.make_async_copy(blocks.at[n], out_hbm.at[:, :, there], sems.at[total + n]))
        leaving[-1].start()
    for copy in leaving:
        copy.wait()


def place_call(me, parts, size, count, width, before):
    numbers = sorted(parts)
    devices, frames = parts[numbers[0]].shape[:2]
    away = pl.BlockSpec(memory_space=pl.ANY)
    total = len(numbers)
    return pl.pallas_call(
        functools.partial(place_kernel, numbers, len(before)),
        out_shape=jax.ShapeDtypeStruct((frames, 2, count * size, width * devices), BF16),
        in_specs=[pl.BlockSpec(memory_space=pltpu.SMEM)] + [away] * (total + len(before)),
        out_specs=away,
        input_output_aliases={1 + total: 0} if before else {},
        scratch_shapes=[
            pltpu.VMEM((total,) + parts[numbers[0]].shape, BF16),
            pltpu.VMEM((total, frames, 2, count, width * devices), BF16),
            pltpu.SemaphoreType.DMA((2 * total,)),
        ],
        compiler_params=pltpu.CompilerParams(vmem_limit_bytes=VMEM_BYTES),
        cost_estimate=pl.CostEstimate(flops=1 << 20, bytes_accessed=4 * 1024 * 1024, transcendentals=0),
    )(me, *[parts[number] for number in numbers], *before)


def pack_kernel(factor_ref, out_ref):
    for rank in range(factor_ref.shape[0]):
        rows = jnp.concatenate([factor_ref[rank, 0].T, factor_ref[rank, 1].T], 0)
        out_ref[rank] = pack(rows, factor_ref.shape[2])[0]


def pack_call(factors):
    ranks, _, count, width = factors.shape
    lines = packing(count, width)[1]
    shape = jax.ShapeDtypeStruct((ranks, lines, LANES), F32)
    return pl.pallas_call(pack_kernel, out_shape=shape)(factors.transpose(0, 1, 3, 2))


def unpack_kernel(packed_ref, out_ref):
    _, _, width, count = out_ref.shape
    for rank in range(out_ref.shape[0]):
        block = unpack([packed_ref[rank]], 2 * count, width)
        out_ref[rank, 0], out_ref[rank, 1] = block[:count].T, block[count:].T


def unpack_call(packed, shape):
    turned = jax.ShapeDtypeStruct(shape[:2] + (shape[3], shape[2]), F32)
    return pl.pallas_call(unpack_kernel, out_shape=turned)(packed).transpose(0, 1, 3, 2)


def mix(temporal_ref, factors, images_ref):
    devices, frames, ranks = temporal_ref.shape
    for device in range(devices):
        for frame in range(frames):
            value = temporal_ref[device, frame, 0] * factors[0]
            for rank in range(1, ranks):
                value = value + temporal_ref[device, frame, rank] * factors[rank]
            images_ref[device, frame] = value.astype(BF16)


def images_kernel(temporal_ref, factor_ref, images_ref):
    mix(temporal_ref, [factor_ref[rank] for rank in range(factor_ref.shape[0])], images_ref)


def update_kernel(temporal_ref, factor_ref, residual_ref, next_ref, images_ref):
    devices, frames, ranks = temporal_ref.shape
    factors = []
    for rank in range(ranks):
        gradient = 0.0
        for frame in range(frames):
            for device in range(devices):
                gradient = gradient + temporal_ref[device, frame, rank] * residual_ref[device, frame]
        factors.append(factor_ref[rank] - STEP_SIZE * gradient)
        next_ref[rank] = factors[rank]
    mix(temporal_ref, factors, images_ref)


def images_call(temporal_all, packed):
    devices, frames, _ = temporal_all.shape
    return pl.pallas_call(
        images_kernel,
        out_shape=jax.ShapeDtypeStruct((devices, frames) + packed.shape[1:], BF16),
        in_specs=[pl.BlockSpec(memory_space=pltpu.SMEM), pl.BlockSpec(memory_space=pltpu.VMEM)],
    )(temporal_all, packed)


def update_call(temporal_all, packed, residual):
    devices, frames, _ = temporal_all.shape
    held = pl.BlockSpec(memory_space=pltpu.VMEM)
    return pl.pallas_call(
        update_kernel,
        out_shape=(
            jax.ShapeDtypeStruct(packed.shape, F32),
            jax.ShapeDtypeStruct((devices, frames) + packed.shape[1:], BF16),
        ),
        in_specs=[pl.BlockSpec(memory_space=pltpu.SMEM)] + [held] * 2,
    )(temporal_all, packed, residual)


def freq_order_rows(rows, period):
    k = np.arange(rows)
    return np.concatenate([k, np.where(k == 0, period // 2, period - k)])


def freq_order_cols(cols, period):
    main = cols // LANES * LANES
    l = np.arange(cols)
    u, v = l, np.where(l == 0, period // 2, period - l)
    return np.concatenate([u[:main], v[:main], u[main:], v[main:]])


def prepare_kernel(index_ref, level_ref, sens_ref, row_ref, col_ref, rev_ref, dup_ref, after_ref, sig_ref, dif_ref, sig0_ref, out_ref):
    frame = pl.program_id(0)
    rows = sig_ref.shape[1]
    half = rows // 2
    levels = level_ref.shape[1]
    scale = 1.0 / (index_ref.shape[1] * index_ref.shape[2])

    def values(index):
        place = dot(index, col_ref[...])
        kernel = jnp.full(place.shape, level_ref[frame, 0] * scale, F32)
        for number in range(1, levels):
            kernel = jnp.where(place > number - 0.5, level_ref[frame, number] * scale, kernel)
        return kernel

    upper = values(index_ref[0, :rows].astype(F32).astype(BF16))
    turned = dot(row_ref[...], index_ref[0, rows:].astype(F32).astype(BF16))
    lower = values(turned.astype(BF16))
    first = lax.broadcasted_iota(jnp.int32, upper[:8].shape, 0) == 0
    sig_ref[0] = upper + lower
    dif_ref[0] = upper - lower
    sig_ref[0, :8] = jnp.where(first, upper[:8], upper[:8] + lower[:8])
    sig0_ref[0] = jnp.where(first, lower[:8], upper[:8] + lower[:8])
    dif_ref[0, :8] = jnp.where(first, 0.0, upper[:8] - lower[:8])

    for part in range(2):
        wide = dot(sens_ref[0, part], dup_ref[...]).astype(BF16)
        out_ref[0, part, :half] = wide[half:]
        out_ref[0, part, half:] = dot(rev_ref[...], wide[:half]).astype(BF16)


def prepare_call(index, level, sens, perms, after):
    frames, rows_pad, cols_pad = index.shape
    coils, _, rows, cols = sens.shape
    row, col, rev, dup = perms
    whole = lambda n: (lambda f: (0,) * n)
    block = lambda *shape: pl.BlockSpec((1,) + shape, lambda f: (f,) + (0,) * len(shape))
    return pl.pallas_call(
        prepare_kernel,
        grid=(frames,),
        out_shape=(
            jax.ShapeDtypeStruct((frames, rows, cols_pad), F32),
            jax.ShapeDtypeStruct((frames, rows, cols_pad), F32),
            jax.ShapeDtypeStruct((frames, 8, cols_pad), F32),
            jax.ShapeDtypeStruct((coils, 2, rows, dup.shape[1]), BF16),
        ),
        in_specs=[
            block(rows_pad, cols_pad),
            pl.BlockSpec(memory_space=pltpu.SMEM),
            block(2, rows, cols),
            pl.BlockSpec(row.shape, whole(2)),
            pl.BlockSpec(col.shape, whole(2)),
            pl.BlockSpec(rev.shape, whole(2)),
            pl.BlockSpec(dup.shape, whole(2)),
            pl.BlockSpec(memory_space=pl.ANY),
        ],
        out_specs=(block(rows, cols_pad), block(rows, cols_pad), block(8, cols_pad), block(2, rows, dup.shape[1])),
        compiler_params=pltpu.CompilerParams(vmem_limit_bytes=VMEM_BYTES),
        cost_estimate=pl.CostEstimate(flops=6 * frames * rows * cols_pad * cols_pad, bytes_accessed=16 * 1024 * 1024, transcendentals=0),
    )(index, level, sens, row, col, rev, dup, after)


def one_hot(order):
    return (order[:, None] == np.arange(len(order))[None, :]).astype(BF16)


def constants(rows, cols, rows_pad, cols_pad):
    assert rows_pad == 2 * rows and cols_pad == 2 * cols
    main = cols // LANES * LANES
    assert 2 * (cols - main) == LANES and rows % 32 == 0
    forward, inverse = row_tables(rows, rows_pad)
    first, last = col_tables(cols, cols_pad)
    turn = np.arange(rows // 2)[::-1]
    flip = freq_order_rows(rows, rows_pad)[rows:] - rows
    spread = np.concatenate([np.arange(cols), np.arange(main, cols)])
    rev, row = one_hot(turn), one_hot(flip)
    col = one_hot(freq_order_cols(cols, cols_pad)).T
    dup = (np.arange(cols)[:, None] == spread[None, :]).astype(BF16)
    tables = [jnp.asarray(t) for t in (first, last, forward, inverse, rev)]
    return tables, [jnp.asarray(t) for t in (row, col, rev, dup)]


def exchange(value, axis, distance):
    size = lax.axis_size(axis)
    return lax.ppermute(value, axis, [(i, i ^ distance) for i in range(size)])


def gather_blocks(own, axis):
    held = {0: own}
    distance = lax.axis_size(axis) // 2
    while distance:
        for key in list(held):
            held[key ^ distance] = exchange(held[key], axis, distance)
        distance //= 2
    return held


def scatter_blocks(blocks, axis):
    held = dict(enumerate(blocks))
    distance = 1
    while distance < lax.axis_size(axis):
        held = {
            key: value + exchange(held[key ^ distance], axis, distance)
            for key, value in held.items()
            if not key & distance
        }
        distance *= 2
    return held[0]


def scatter_direct(blocks, axis):
    total = blocks[0]
    for distance in range(1, lax.axis_size(axis)):
        total = total + exchange(blocks[distance], axis, distance)
    return total


def gather_small(value, axis):
    size = lax.axis_size(axis)
    me = lax.axis_index(axis)
    held = value[None]
    distance = 1
    while distance < size:
        other = exchange(held, axis, distance)
        upper = (me // distance) % 2 == 1
        held = jnp.where(upper, jnp.concatenate([other, held]), jnp.concatenate([held, other]))
        distance *= 2
    return held


def swap(value):
    return lax.all_to_all(value, "frame", split_axis=0, concat_axis=0, tiled=True)


def body(spatial, temporal, sensitivity, coil_data, kernel_index, kernel_level):
    rows, cols = sensitivity.shape[2:]
    tables, perms = constants(rows, cols, kernel_index.shape[1], kernel_index.shape[2])
    me = lax.axis_index("coil").astype(jnp.int32)[None]
    size = lax.axis_size("coil")
    temporal_all = gather_small(temporal, "frame")
    packed = pack_call(spatial)
    images = images_call(temporal_all, packed)
    own = swap(images)
    frames = own.shape[1]

    sig, dif, sig0, wide = prepare_call(kernel_index, kernel_level, sensitivity, perms, images)
    held = gather_blocks(own, "coil")
    parts = [held[number] for number in range(size)]
    blocks = []
    coils = range(sensitivity.shape[0])
    for frame in range(frames):
        before = blocks[-1][:1] if blocks else []
        blocks.append(normal_call(frame, coils, me, parts, wide, sig, dif, sig0, coil_data, tables, before))
    sums = []
    for frame in range(frames):
        sums.append((scatter_blocks if frame == frames - 1 else scatter_direct)(blocks[frame], "coil"))
    residual = swap(jnp.stack(sums, 1))
    packed_next, images = update_call(temporal_all, packed, residual)
    own = swap(images)
    spatial_next = unpack_call(packed_next, spatial.shape)
    held = gather_blocks(own, "coil")
    out = []
    for chosen in (range(size // 2), range(size // 2, size)):
        group = {number: held[number] for number in chosen}
        out = [place_call(me, group, size, spatial.shape[2], spatial.shape[3], out)]
    return spatial_next, out[0]


def solution(mesh):
    placed = (
        P(None, None, "coil", "frame"),
        P("frame", None),
        P("coil", None, None, None),
        P("frame", "coil", None, None, None),
        P("frame", None, None),
        P("frame", None),
    )
    return jax.shard_map(
        body,
        mesh=mesh,
        in_specs=placed,
        out_specs=(P(None, None, "coil", "frame"), P("frame", None, None, None)),
        check_vma=False,
    )
```

```python
import functools
import jax, jax.numpy as jnp, numpy as np
from jax import lax
from jax.sharding import PartitionSpec as P
from jax.experimental import pallas as pl
from jax.experimental.pallas import tpu as pltpu

STEP_SIZE = 0.15
LANES = 128
VMEM_BYTES = 67043328
F32, BF16 = jnp.float32, jnp.bfloat16


def halves(table):
    high = np.asarray(table, np.float32).astype(BF16)
    low = (table - high.astype(np.float64)).astype(np.float32).astype(BF16)
    return high, low


def wave(count, places, period):
    turns = np.outer(np.arange(count), places) % (2 * period)
    slot = np.outer([period // 2], places) % (2 * period)
    angle = np.pi / period * turns
    cosine, sine = np.cos(angle), np.sin(angle)
    sine[0] = np.sin(np.pi / period * slot[0])
    return cosine, sine


def row_tables(rows, period):
    cosine, sine = wave(rows, 2 * np.arange(rows // 2) + 1, period)
    forward, inverse = [], []
    for table in (cosine, sine):
        high, low = halves(table)
        forward.append(np.concatenate([high, high, low], 1))
        inverse.append(np.concatenate([high.T, high.T, low.T], 1))
    return np.stack(forward), np.stack(inverse)


def col_tables(cols, period):
    main = cols // LANES * LANES
    cosine, sine = wave(cols, 2 * np.arange(cols) - (cols - 1), period)
    mixed = np.concatenate([cosine[:main], sine[:main], cosine[main:], sine[main:]], 0).T
    high, low = halves(mixed)
    blank = np.zeros((cols - main, mixed.shape[1]), BF16)
    forward = np.concatenate([high[:main], high[:main], low[:main], high[main:], high[main:], low[main:], blank], 0)
    high, low = high.T, low.T
    inverse = np.concatenate([high, high, low], 0)
    return forward, inverse


def split(value):
    high = value.astype(BF16)
    return high, (value - high.astype(F32)).astype(BF16)


def dot(left, right):
    return jnp.dot(left, right, preferred_element_type=F32)


def packing(count, width):
    groups = LANES // width
    lines = -(-2 * count // groups)
    return groups, -(-lines // 8) * 8


def pack(rows, width):
    total, cols = rows.shape
    groups, lines = packing(total // 2, width)
    missing = groups * lines - total
    if missing:
        rows = jnp.concatenate([rows, jnp.zeros((missing, cols), rows.dtype)], 0)
    rest = LANES - groups * width
    packed = []
    for at in range(0, cols, width):
        pieces = [rows[g * lines : (g + 1) * lines, at : at + width] for g in range(groups)]
        if rest:
            pieces.append(jnp.zeros((lines, rest), rows.dtype))
        packed.append(jnp.concatenate(pieces, 1))
    return packed


def unpack(packed, total, width):
    groups, _ = packing(total // 2, width)
    bands = [jnp.concatenate([p[:, g * width : (g + 1) * width] for p in packed], 1) for g in range(groups)]
    return jnp.concatenate(bands, 0)[:total]


def normal_kernel(size, extra, frame, first_coil, me_ref, *refs):
    parts_hbm, refs = refs[:size], refs[size:]
    sens_hbm, sig_hbm, dif_hbm, data_hbm, tcol_hbm, trow_hbm, tback_hbm, tlast_hbm, sig0_ref, rev_ref = refs[:10]
    before, refs = refs[10 : 10 + extra], refs[10 + extra :]
    blocks, refs = refs[:size], refs[size:]
    sens_ref, tcol_ref, trow_ref, sig_ref, dif_ref, tback_ref, tlast_ref, data_ref, sems = refs[:9]
    parts, img_n, img_s, xcat, mid, back, last, acc = refs[9:]
    arrived = [pltpu.make_async_copy(parts_hbm[n].at[:, frame], parts.at[n], sems.at[8 + n]) for n in range(size)]
    for copy in arrived:
        copy.start()
    chosen = pl.ds(first_coil, sens_ref.shape[0])
    moved = [
        pltpu.make_async_copy(source, target, sems.at[n])
        for n, (source, target) in enumerate((
            (sens_hbm.at[chosen], sens_ref), (tcol_hbm, tcol_ref), (trow_hbm, trow_ref), (sig_hbm.at[frame], sig_ref), (dif_hbm.at[frame], dif_ref),
            (tback_hbm, tback_ref), (tlast_hbm, tlast_ref), (data_hbm.at[frame, chosen], data_ref),
        ))
    ]
    for copy in moved:
        copy.start()
    coils, _, rows, _ = sens_ref.shape
    cols = acc.shape[2]
    half = rows // 2
    main = cols // LANES * LANES
    spectral = tcol_ref.shape[1]
    steps = spectral // LANES
    count = rows // size

    def place(number):
        return pl.ds(pl.multiple_of((me_ref[0] ^ number) * count, count), count)

    width = cols // parts.shape[1]
    for number in range(size):
        arrived[number].wait()
        block = unpack([parts[number, n].astype(F32) for n in range(cols // width)], 2 * count, width)
        for part in range(2):
            img_n[part, place(number)] = block[part * count : (part + 1) * count].astype(BF16)
    for part in range(2):
        for top, value in enumerate((img_n[part, half:].astype(F32), dot(rev_ref[...], img_n[part, :half]))):
            here = slice(top * half, top * half + half)
            img_s[part, here, :main] = value[:, :main]
            img_s[part, here, main:] = jnp.concatenate([value[:, main:]] * (LANES // (cols - main)), 1)
    moved[0].wait()
    lane = lax.broadcasted_iota(jnp.int32, (half, LANES), 1)
    keep = (lane > 0).astype(F32)
    low_lane = lane < (cols - main)

    def fold(coil):
        sums = {}
        for top in range(2):
            here = slice(top * half, top * half + half)
            s_re = sens_ref[coil, 0, here].astype(F32)
            s_im = sens_ref[coil, 1, here].astype(F32)
            i_re, i_im = img_s[0, here], img_s[1, here]
            sums[top, 0] = s_re * i_re - s_im * i_im
            sums[top, 1] = s_re * i_im + s_im * i_re
        for part in range(2):
            for sign in range(2):
                value = sums[0, part] + sums[1, part] if sign == 0 else sums[0, part] - sums[1, part]
                high, low = split(value)
                there = slice((2 * sign + part) * half, (2 * sign + part + 1) * half)
                xcat[coil, there, :main] = high[:, :main]
                xcat[coil, there, main : 2 * main] = low[:, :main]
                xcat[coil, there, 2 * main : 2 * main + LANES] = jnp.where(low_lane, high[:, main:], low[:, main:])
                xcat[coil, there, 2 * main + LANES :] = high[:, main:]

    def columns(coil):
        products = []
        for sign in range(2):
            lines = slice(2 * sign * half, (2 * sign + 2) * half)
            spread = [xcat[coil, lines, : 2 * main], xcat[coil, lines, :main], xcat[coil, lines, 2 * main :]]
            products.append(dot(jnp.concatenate(spread, 1), tcol_ref[...]))
        return products

    def mix_columns(coil, products):
        for sign in range(2):
            both = products[sign]
            re, im = both[:half], both[half:]
            for step in range(steps):
                at = step * LANES
                if at < main:
                    c_re, c_im = re[:, at : at + LANES], im[:, at : at + LANES]
                    s_re, s_im = re[:, main + at : main + at + LANES], im[:, main + at : main + at + LANES]
                    if at == 0:
                        s_re, s_im = s_re * keep, s_im * keep
                    m_re, m_im = c_re + s_im, c_im - s_re
                elif at < 2 * main:
                    c_re, c_im = re[:, at - main : at - main + LANES], im[:, at - main : at - main + LANES]
                    s_re, s_im = re[:, at : at + LANES], im[:, at : at + LANES]
                    if at == main:
                        c_re, c_im = c_re * keep, c_im * keep
                    m_re, m_im = c_re - s_im, c_im + s_re
                else:
                    g_re, g_im = re[:, at : at + LANES], im[:, at : at + LANES]
                    m_re = g_re + pltpu.roll(g_im, LANES // 2, 1)
                    m_im = g_im - pltpu.roll(g_re, LANES // 2, 1)
                for part, value in enumerate((m_re, m_im)):
                    high, low = split(value)
                    there = slice((2 * step + part) * LANES, (2 * step + part + 1) * LANES)
                    mid[coil, sign, :half, there] = high
                    mid[coil, sign, half:, there] = low


    def rows_pass(coil):
        def forward(step):
            there = slice(step * 2 * LANES, (step + 1) * 2 * LANES)
            return [
                dot(trow_ref[sign], jnp.concatenate([mid[coil, sign, :, there], mid[coil, sign, :half, there]], 0)) for sign in range(2)
            ]

        following = forward(0)
        for step in range(steps):
            there = slice(step * 2 * LANES, (step + 1) * 2 * LANES)
            here = slice(step * LANES, (step + 1) * LANES)
            even, odd = following
            if step + 1 < steps:
                following = forward(step + 1)
            sig, dif = sig_ref[:, here], dif_ref[:, here]
            c_re, c_im = even[:, :LANES], even[:, LANES:]
            s_re, s_im = odd[:, :LANES], odd[:, LANES:]
            p_re = sig * c_re + dif * s_im
            p_im = sig * c_im - dif * s_re
            q_re = sig * s_re - dif * c_im
            q_im = sig * s_im + dif * c_re
            first = sig0_ref[frame, :, here]
            q_re = jnp.concatenate([first * s_re[:8] - dif[:8] * c_im[:8], q_re[8:]], 0)
            q_im = jnp.concatenate([first * s_im[:8] + dif[:8] * c_re[:8], q_im[8:]], 0)
            for number, pair in enumerate(((p_re, p_im), (q_re, q_im))):
                both = [split(value) for value in pair]
                high, low = [jnp.concatenate([both[0][n], both[1][n]], 1) for n in range(2)]
                back[coil, number, :, there] = dot(tback_ref[number], jnp.concatenate([high, low, high], 0))

    def unmix_columns(coil):
        for sign in range(2):
            for step in range(steps):
                at = step * LANES

                def piece(index, part):
                    return back[coil, sign, :, (2 * index + part) * LANES : (2 * index + part + 1) * LANES]

                shift = main // LANES
                if at < main:
                    u_re, u_im = piece(step, 0), piece(step, 1)
                    v_re, v_im = piece(step + shift, 0), piece(step + shift, 1)
                    if at == 0:
                        v_re, v_im = v_re * keep, v_im * keep
                    w_re, w_im = u_re + v_re, u_im + v_im
                elif at < 2 * main:
                    u_re, u_im = piece(step - shift, 0), piece(step - shift, 1)
                    v_re, v_im = piece(step, 0), piece(step, 1)
                    if at == main:
                        u_re, u_im = u_re * keep, u_im * keep
                    w_re, w_im = v_im - u_im, u_re - v_re
                else:
                    g_re, g_im = piece(step, 0), piece(step, 1)
                    w_re = g_re - pltpu.roll(g_im, LANES // 2, 1)
                    w_im = g_im + pltpu.roll(g_re, LANES // 2, 1)
                for part, value in enumerate((w_re, w_im)):
                    high, low = split(value)
                    there = slice((2 * sign + part) * half, (2 * sign + part + 1) * half)
                    last[coil, there, at : at + LANES] = high
                    last[coil, there, spectral + at : spectral + at + LANES] = low

    def last_columns(coil):
        return dot(jnp.concatenate([last[coil], last[coil, :, :spectral]], 1), tlast_ref[...])

    def add_residual(coil, final):
        plus_re, plus_im, minus_re, minus_im = [final[n * half : (n + 1) * half] for n in range(4)]
        for top in range(2):
            here = slice(top * half, top * half + half)
            n_re = plus_re + minus_re if top == 0 else plus_re - minus_re
            n_im = plus_im + minus_im if top == 0 else plus_im - minus_im
            if top == 0:
                d_re, d_im = data_ref[coil, 0, half:].astype(F32), data_ref[coil, 1, half:].astype(F32)
            else:
                d_re, d_im = dot(rev_ref[...], data_ref[coil, 0, :half]), dot(rev_ref[...], data_ref[coil, 1, :half])
            n_re, n_im = n_re - d_re, n_im - d_im
            s_re = sens_ref[coil, 0, here, :cols].astype(F32)
            s_im = sens_ref[coil, 1, here, :cols].astype(F32)
            acc[0, here] += s_re * n_re + s_im * n_im
            acc[1, here] += s_re * n_im - s_im * n_re

    acc[...] = jnp.zeros_like(acc)
    fold(0)
    moved[1].wait()
    products = columns(0)
    for coil in range(coils):
        if coil + 1 < coils:
            fold(coil + 1)
        mix_columns(coil, products)
        if coil == 0:
            for copy in moved[2:6]:
                copy.wait()
        rows_pass(coil)
        if coil + 1 < coils:
            products = columns(coil + 1)
        unmix_columns(coil)
        if coil == 0:
            moved[6].wait()
            moved[7].wait()
        add_residual(coil, last_columns(coil))
    for part in range(2):
        above, below = acc[part, :half], acc[part, half:]
        high, low = split(below)
        rest = (below - high.astype(F32) - low.astype(F32)).astype(BF16)
        turned = dot(rev_ref[...], high) + dot(rev_ref[...], low) + dot(rev_ref[...], rest)
        acc[part, half:] = above
        acc[part, :half] = turned
    for number in range(size):
        block = jnp.concatenate([acc[part, place(number)] for part in range(2)], 0)
        for n, value in enumerate(pack(block, width)):
            blocks[number][n] = value + before[number][n] if extra == size else value


def normal_call(frame, chosen, me, parts, sens, sig, dif, sig0, data, tables, before):
    size = len(parts)
    rows, wide = sens.shape[2:]
    coils = len(chosen)
    cols = data.shape[4]
    half = rows // 2
    tcol, tlast, trow, tback, rev = tables
    spectral = tcol.shape[1]
    held = pl.BlockSpec(memory_space=pltpu.VMEM)
    away = pl.BlockSpec(memory_space=pl.ANY)
    like = lambda value: pltpu.VMEM(value.shape, value.dtype)
    one = lambda value: pltpu.VMEM(value.shape[1:], value.dtype)
    some = lambda value: pltpu.VMEM((coils,) + value.shape[1:], value.dtype)
    packed = parts[0].shape[:1] + parts[0].shape[2:]
    flops = 2 * coils * 2 * 12 * rows * cols * spectral

    return pl.pallas_call(
        functools.partial(normal_kernel, size, len(before), frame, chosen[0]),
        out_shape=[jax.ShapeDtypeStruct(packed, F32)] * size,
        in_specs=[pl.BlockSpec(memory_space=pltpu.SMEM)] + [away] * (size + 8) + [held] * 2 + [held if len(before) == size else away] * len(before),
        out_specs=[held] * size,
        scratch_shapes=[
            some(sens), like(tcol), like(trow), one(sig), one(dif), like(tback), like(tlast), some(one(data)),
            pltpu.SemaphoreType.DMA((8 + size,)),
            pltpu.VMEM((size,) + packed, BF16),
            pltpu.VMEM((2, rows, cols), BF16),
            pltpu.VMEM((2, rows, wide), F32),
            pltpu.VMEM((coils, 4 * half, tcol.shape[0] * 3 // 4), BF16),
            pltpu.VMEM((coils, 2, 2 * half, 2 * spectral), BF16),
            pltpu.VMEM((coils, 2, half, 2 * spectral), F32),
            pltpu.VMEM((coils, 4 * half, 2 * spectral), BF16),
            pltpu.VMEM((2, rows, cols), F32),
        ],
        compiler_params=pltpu.CompilerParams(vmem_limit_bytes=VMEM_BYTES - (9 << 17)),
        cost_estimate=pl.CostEstimate(flops=flops, bytes_accessed=8 * 1024 * 1024, transcendentals=0),
    )(me, *parts, sens, sig, dif, data, tcol, trow, tback, tlast, sig0, rev, *before)


def place_kernel(numbers, extra, me_ref, *refs):
    total = len(numbers)
    parts_in, out_hbm = refs[:total], refs[total + extra]
    blocks, sems = refs[total + extra + 1 :]
    devices, frames = parts_in[0].shape[:2]
    count = blocks.shape[3]
    width = blocks.shape[4] // devices
    leaving = []
    for n, number in enumerate(numbers):
        for frame in range(frames):
            block = unpack([parts_in[n][device, frame].astype(F32) for device in range(devices)], 2 * count, width)
            for part in range(2):
                blocks[n, frame, part] = block[part * count : (part + 1) * count].astype(BF16)
        there = pl.ds(pl.multiple_of((me_ref[0] ^ number) * count, count), count)
        leaving.append(pltpu.make_async_copy(blocks.at[n], out_hbm.at[:, :, there], sems.at[n]))
        leaving[-1].start()
    for copy in leaving:
        copy.wait()


def place_call(me, parts, size, count, width, before):
    numbers = sorted(parts)
    devices, frames = parts[numbers[0]].shape[:2]
    away = pl.BlockSpec(memory_space=pl.ANY)
    held = pl.BlockSpec(memory_space=pltpu.VMEM)
    total = len(numbers)
    return pl.pallas_call(
        functools.partial(place_kernel, numbers, len(before)),
        out_shape=jax.ShapeDtypeStruct((frames, 2, count * size, width * devices), BF16),
        in_specs=[pl.BlockSpec(memory_space=pltpu.SMEM)] + [held] * total + [away] * len(before),
        out_specs=away,
        input_output_aliases={1 + total: 0} if before else {},
        scratch_shapes=[
            pltpu.VMEM((total, frames, 2, count, width * devices), BF16),
            pltpu.SemaphoreType.DMA((total,)),
        ],
        compiler_params=pltpu.CompilerParams(vmem_limit_bytes=VMEM_BYTES // 4),
        cost_estimate=pl.CostEstimate(flops=1 << 20, bytes_accessed=4 * 1024 * 1024, transcendentals=0),
    )(me, *[parts[number] for number in numbers], *before)


def pack_kernel(factor_ref, out_ref):
    for rank in range(factor_ref.shape[0]):
        rows = jnp.concatenate([factor_ref[rank, 0].T, factor_ref[rank, 1].T], 0)
        out_ref[rank] = pack(rows, factor_ref.shape[2])[0]


def pack_call(factors):
    ranks, _, count, width = factors.shape
    lines = packing(count, width)[1]
    shape = jax.ShapeDtypeStruct((ranks, lines, LANES), F32)
    return pl.pallas_call(pack_kernel, out_shape=shape)(factors.transpose(0, 1, 3, 2))


def unpack_kernel(packed_ref, out_ref):
    _, _, width, count = out_ref.shape
    for rank in range(out_ref.shape[0]):
        block = unpack([packed_ref[rank]], 2 * count, width)
        out_ref[rank, 0], out_ref[rank, 1] = block[:count].T, block[count:].T


def unpack_call(packed, shape):
    turned = jax.ShapeDtypeStruct(shape[:2] + (shape[3], shape[2]), F32)
    return pl.pallas_call(unpack_kernel, out_shape=turned)(packed).transpose(0, 1, 3, 2)


def mix(temporal_ref, factors, images_ref):
    devices, frames, ranks = temporal_ref.shape
    for device in range(devices):
        for frame in range(frames):
            value = temporal_ref[device, frame, 0] * factors[0]
            for rank in range(1, ranks):
                value = value + temporal_ref[device, frame, rank] * factors[rank]
            images_ref[device, frame] = value.astype(BF16)


def images_kernel(temporal_ref, factor_ref, images_ref):
    mix(temporal_ref, [factor_ref[rank] for rank in range(factor_ref.shape[0])], images_ref)


def update_kernel(temporal_ref, factor_ref, residual_ref, next_ref, images_ref):
    devices, frames, ranks = temporal_ref.shape
    factors = []
    for rank in range(ranks):
        gradient = 0.0
        for frame in range(frames):
            for device in range(devices):
                gradient = gradient + temporal_ref[device, frame, rank] * residual_ref[device, frame]
        factors.append(factor_ref[rank] - STEP_SIZE * gradient)
        next_ref[rank] = factors[rank]
    mix(temporal_ref, factors, images_ref)


def images_call(temporal_all, packed):
    devices, frames, _ = temporal_all.shape
    return pl.pallas_call(
        images_kernel,
        out_shape=jax.ShapeDtypeStruct((devices, frames) + packed.shape[1:], BF16),
        in_specs=[pl.BlockSpec(memory_space=pltpu.SMEM), pl.BlockSpec(memory_space=pltpu.VMEM)],
    )(temporal_all, packed)


def update_call(temporal_all, packed, residual):
    devices, frames, _ = temporal_all.shape
    held = pl.BlockSpec(memory_space=pltpu.VMEM)
    return pl.pallas_call(
        update_kernel,
        out_shape=(
            jax.ShapeDtypeStruct(packed.shape, F32),
            jax.ShapeDtypeStruct((devices, frames) + packed.shape[1:], BF16),
        ),
        in_specs=[pl.BlockSpec(memory_space=pltpu.SMEM)] + [held] * 2,
    )(temporal_all, packed, residual)


def freq_order_rows(rows, period):
    k = np.arange(rows)
    return np.concatenate([k, np.where(k == 0, period // 2, period - k)])


def freq_order_cols(cols, period):
    main = cols // LANES * LANES
    l = np.arange(cols)
    u, v = l, np.where(l == 0, period // 2, period - l)
    return np.concatenate([u[:main], v[:main], u[main:], v[main:]])


def prepare_kernel(index_ref, level_ref, sens_ref, row_ref, col_ref, rev_ref, dup_ref, after_ref, sig_ref, dif_ref, sig0_ref, out_ref):
    frame = pl.program_id(0)
    rows = sig_ref.shape[1]
    half = rows // 2
    levels = level_ref.shape[1]
    scale = 1.0 / (index_ref.shape[1] * index_ref.shape[2])

    def values(index):
        place = dot(index, col_ref[...])
        kernel = jnp.full(place.shape, level_ref[frame, 0] * scale, F32)
        for number in range(1, levels):
            kernel = jnp.where(place > number - 0.5, level_ref[frame, number] * scale, kernel)
        return kernel

    upper = values(index_ref[0, :rows].astype(F32).astype(BF16))
    turned = dot(row_ref[...], index_ref[0, rows:].astype(F32).astype(BF16))
    lower = values(turned.astype(BF16))
    first = lax.broadcasted_iota(jnp.int32, upper[:8].shape, 0) == 0
    sig_ref[0] = upper + lower
    dif_ref[0] = upper - lower
    sig_ref[0, :8] = jnp.where(first, upper[:8], upper[:8] + lower[:8])
    sig0_ref[0] = jnp.where(first, lower[:8], upper[:8] + lower[:8])
    dif_ref[0, :8] = jnp.where(first, 0.0, upper[:8] - lower[:8])

    for part in range(2):
        wide = dot(sens_ref[0, part], dup_ref[...]).astype(BF16)
        out_ref[0, part, :half] = wide[half:]
        out_ref[0, part, half:] = dot(rev_ref[...], wide[:half]).astype(BF16)


def prepare_call(index, level, sens, perms, after):
    frames, rows_pad, cols_pad = index.shape
    coils, _, rows, cols = sens.shape
    row, col, rev, dup = perms
    whole = lambda n: (lambda f: (0,) * n)
    block = lambda *shape: pl.BlockSpec((1,) + shape, lambda f: (f,) + (0,) * len(shape))
    return pl.pallas_call(
        prepare_kernel,
        grid=(frames,),
        out_shape=(
            jax.ShapeDtypeStruct((frames, rows, cols_pad), F32),
            jax.ShapeDtypeStruct((frames, rows, cols_pad), F32),
            jax.ShapeDtypeStruct((frames, 8, cols_pad), F32),
            jax.ShapeDtypeStruct((coils, 2, rows, dup.shape[1]), BF16),
        ),
        in_specs=[
            block(rows_pad, cols_pad),
            pl.BlockSpec(memory_space=pltpu.SMEM),
            block(2, rows, cols),
            pl.BlockSpec(row.shape, whole(2)),
            pl.BlockSpec(col.shape, whole(2)),
            pl.BlockSpec(rev.shape, whole(2)),
            pl.BlockSpec(dup.shape, whole(2)),
            pl.BlockSpec(memory_space=pl.ANY),
        ],
        out_specs=(block(rows, cols_pad), block(rows, cols_pad), block(8, cols_pad), block(2, rows, dup.shape[1])),
        compiler_params=pltpu.CompilerParams(vmem_limit_bytes=VMEM_BYTES),
        cost_estimate=pl.CostEstimate(flops=6 * frames * rows * cols_pad * cols_pad, bytes_accessed=16 * 1024 * 1024, transcendentals=0),
    )(index, level, sens, row, col, rev, dup, after)


def one_hot(order):
    return (order[:, None] == np.arange(len(order))[None, :]).astype(BF16)


def constants(rows, cols, rows_pad, cols_pad):
    assert rows_pad == 2 * rows and cols_pad == 2 * cols
    main = cols // LANES * LANES
    assert 2 * (cols - main) == LANES and rows % 32 == 0
    forward, inverse = row_tables(rows, rows_pad)
    first, last = col_tables(cols, cols_pad)
    turn = np.arange(rows // 2)[::-1]
    flip = freq_order_rows(rows, rows_pad)[rows:] - rows
    spread = np.concatenate([np.arange(cols), np.arange(main, cols)])
    rev, row = one_hot(turn), one_hot(flip)
    col = one_hot(freq_order_cols(cols, cols_pad)).T
    dup = (np.arange(cols)[:, None] == spread[None, :]).astype(BF16)
    tables = [jnp.asarray(t) for t in (first, last, forward, inverse, rev)]
    return tables, [jnp.asarray(t) for t in (row, col, rev, dup)]


def exchange(value, axis, distance):
    size = lax.axis_size(axis)
    return lax.ppermute(value, axis, [(i, i ^ distance) for i in range(size)])


def gather_blocks(own, axis):
    held = {0: own}
    distance = lax.axis_size(axis) // 2
    while distance:
        for key in list(held):
            held[key ^ distance] = exchange(held[key], axis, distance)
        distance //= 2
    return held


def scatter_blocks(blocks, axis):
    held = dict(enumerate(blocks))
    distance = 1
    while distance < lax.axis_size(axis):
        held = {
            key: value + exchange(held[key ^ distance], axis, distance)
            for key, value in held.items()
            if not key & distance
        }
        distance *= 2
    return held[0]


def scatter_direct(blocks, axis):
    total = blocks[0]
    for distance in range(1, lax.axis_size(axis)):
        total = total + exchange(blocks[distance], axis, distance)
    return total


def gather_small(value, axis):
    size = lax.axis_size(axis)
    me = lax.axis_index(axis)
    held = value[None]
    distance = 1
    while distance < size:
        other = exchange(held, axis, distance)
        upper = (me // distance) % 2 == 1
        held = jnp.where(upper, jnp.concatenate([other, held]), jnp.concatenate([held, other]))
        distance *= 2
    return held


def swap(value):
    return lax.all_to_all(value, "frame", split_axis=0, concat_axis=0, tiled=True)


def body(spatial, temporal, sensitivity, coil_data, kernel_index, kernel_level):
    rows, cols = sensitivity.shape[2:]
    tables, perms = constants(rows, cols, kernel_index.shape[1], kernel_index.shape[2])
    me = lax.axis_index("coil").astype(jnp.int32)[None]
    size = lax.axis_size("coil")
    temporal_all = gather_small(temporal, "frame")
    packed = pack_call(spatial)
    images = images_call(temporal_all, packed)
    own = swap(images)
    frames = own.shape[1]

    sig, dif, sig0, wide = prepare_call(kernel_index, kernel_level, sensitivity, perms, images)
    held = gather_blocks(own, "coil")
    parts = [held[number] for number in range(size)]
    blocks = []
    coils = range(sensitivity.shape[0])
    for frame in range(frames):
        before = blocks[-1][:1] if blocks else []
        blocks.append(normal_call(frame, coils, me, parts, wide, sig, dif, sig0, coil_data, tables, before))
    sums = []
    for frame in range(frames):
        sums.append((scatter_blocks if frame == frames - 1 else scatter_direct)(blocks[frame], "coil"))
    residual = swap(jnp.stack(sums, 1))
    packed_next, images = update_call(temporal_all, packed, residual)
    own = swap(images)
    spatial_next = unpack_call(packed_next, spatial.shape)
    held = gather_blocks(own, "coil")
    out = []
    for chosen in (range(size // 2), range(size // 2, size)):
        group = {number: held[number] for number in chosen}
        out = [place_call(me, group, size, spatial.shape[2], spatial.shape[3], out)]
    return spatial_next, out[0]


def solution(mesh):
    placed = (
        P(None, None, "coil", "frame"),
        P("frame", None),
        P("coil", None, None, None),
        P("frame", "coil", None, None, None),
        P("frame", None, None),
        P("frame", None),
    )
    return jax.shard_map(
        body,
        mesh=mesh,
        in_specs=placed,
        out_specs=(P(None, None, "coil", "frame"), P("frame", None, None, None)),
        check_vma=False,
    )
```
